32 devices in a mesh: query: 2 (over y), dom: 16 (over z, x, core).
Axes of the slice: x: 2, y: 2, z: 4, core: 2. Of those that a mesh axis runs over, the one named last changes fastest.
Arguments:
- h_in: bfloat16 [4096, 256], P('dom', 'query'), may hold values from -6 to 6
- cotangent: bfloat16 [4096, 256], P('dom', 'query'), may hold values from -6 to 6
- w_one: bfloat16 [64, 64], replicated, may hold values from -0.75 to 0.75
- w_two: bfloat16 [64, 64], replicated, may hold values from -0.75 to 0.75
- rel_one: bfloat16 [535, 64], replicated, may hold values from -3 to 3
- rel_two: bfloat16 [535, 64], replicated, may hold values from -3 to 3
- query_emb: bfloat16 [535, 64], replicated, may hold values from -6 to 6
- q_head: int32 [4], P('query'), may hold values from 0 to 4095
- q_rel: int32 [4], P('query'), may hold values from 0 to 534
- bnd_rows: int32 [1024], P('dom'), may hold values from 0 to 255
- ghost_slots: int32 [256, 16], P('dom'), may hold values from 0 to 63
- edges_in: int32 [3, 16384], P(None, 'dom'), may hold values from 0 to 535, as said below
- edges_bd: int32 [3, 16384], P(None, 'dom'), may hold values from 0 to 535, as said below
Outputs:
- grad_in: float32 [4096, 256], P('dom', 'query')
- grad_w: float32 [2, 64, 64], replicated
- grad_rel: float32 [2, 535, 64], replicated
The draws below stay inside these ranges and needn't reach their ends.
Inputs may be any that keep to these rules, and one draw needn't show every extreme that they name: `edges_in`: row 0 is a local source row, row 1 a local destination row, row 2 a relation; relation 535 marks padding, which follows all real edges in each partition's block of 1024; at least a quarter of each block is real and some partition's block has no padding. `edges_bd`: row 0 is a ghost index below 256, row 1 a local destination row, row 2 a relation; relation 535 marks padding, which follows all real edges in each partition's block of 1024; at least a quarter of each block is real and some partition's block has no padding.
All inputs are finite; a program needn't handle non-finite values.
Results may differ from the reference program's by a relative error of at most 0.0049.
The reference program's roundings to bfloat16 on the way count: a program that leaves them out, or rounds other values in their place, can miss the bound.
Values may be sent and summed in bfloat16 or wider, within the bound.
A program may use at most 64 MiB of HBM per device.

```python
import jax
import jax.numpy as jnp
from jax import lax

D = 64
NREL = 535
ENT_DEV = 256
EIN = 1024
EBD = 1024
SEND = 16
BND = 64
ENTITIES = 4096
QUERIES = 4
N_DOM = 16


def edge_block(key, per_device, source_top, salt_code):
    folded = jax.random.fold_in(key, salt_code)
    subkeys = jax.random.split(folded, 5)
    source = jax.random.randint(subkeys[0], (N_DOM, per_device), 0, source_top)
    target = jax.random.randint(subkeys[1], (N_DOM, per_device), 0, ENT_DEV)
    relation = jax.random.randint(subkeys[2], (N_DOM, per_device), 0, NREL)
    alive = jax.random.randint(subkeys[3], (N_DOM,), max(per_device // 4, 1), per_device + 1)
    filled = jax.random.randint(subkeys[4], (), 0, N_DOM)
    alive = jnp.where(jnp.arange(N_DOM) == filled, per_device, alive)
    places = jnp.arange(per_device)
    relation = jnp.where(places[None, :] < alive[:, None], relation, NREL)
    return jnp.stack([source, target, relation]).reshape(3, N_DOM * per_device).astype(jnp.int32)


def draw_edges_in(key, part):
    return edge_block(key, EIN, ENT_DEV, 11)


def draw_edges_bd(key, part):
    return edge_block(key, EBD, N_DOM * SEND, 23)


def with_ends(drawn, rng, least, high):
    shape = drawn.shape
    spot = [jax.random.randint(jax.random.fold_in(rng, axis), (), 0, shape[axis]) for axis in range(len(shape))]
    drawn = drawn.at[tuple(spot)].set(least)
    longest = shape.index(max(shape))
    spot[longest] = (spot[longest] + 1) % shape[longest]
    return drawn.at[tuple(spot)].set(high)


def steps_of(key, dims, shards, smallest, largest):
    gain = 1.0
    for axis_at, blocks in shards:
        draws = jax.random.uniform(jax.random.fold_in(jax.random.fold_in(key, 6), axis_at), (blocks,), jnp.float32, smallest / len(shards), largest / len(shards))
        gain = gain * jnp.repeat(jnp.exp(draws), dims[axis_at] // blocks).reshape((-1,) + (1,) * (len(dims) - 1 - axis_at))
    return gain


def centred(rng, shape, scale, most, pieces=(), kind=jnp.bfloat16):
    factor_of = steps_of(rng, shape, pieces, -0.22, 0.18) if pieces else 1.0
    array = jax.random.normal(rng, shape, jnp.float32) * scale * factor_of
    return jnp.minimum(jnp.maximum(array, -most), most).astype(kind)


def setup_inputs(seed: int = 0) -> dict:
    seeds = jax.random.split(jax.random.key(seed), 14)
    h_in = centred(seeds[0], (ENTITIES, QUERIES * D), 1.0, 6.0, ((0, 16), (1, 2)))
    cotangent = centred(seeds[1], (ENTITIES, QUERIES * D), 1.0, 6.0, ((0, 16), (1, 2)))
    w_one = centred(seeds[2], (D, D), D ** -0.5, 0.75)
    w_two = centred(seeds[3], (D, D), D ** -0.5, 0.75)
    rel_one = centred(seeds[4], (NREL, D), 0.5, 3.0)
    rel_two = centred(seeds[5], (NREL, D), 0.5, 3.0)
    query_emb = centred(seeds[6], (NREL, D), 1.0, 6.0)
    q_head = with_ends(jax.random.randint(seeds[7], (QUERIES,), 0, ENTITIES), jax.random.fold_in(seeds[7], 1), 0, ENTITIES - 1).astype(jnp.int32)
    q_rel = with_ends(jax.random.randint(seeds[8], (QUERIES,), 0, NREL), jax.random.fold_in(seeds[8], 1), 0, NREL - 1).astype(jnp.int32)
    bnd_rows = with_ends(jax.random.randint(seeds[9], (N_DOM * BND,), 0, ENT_DEV), jax.random.fold_in(seeds[9], 1), 0, ENT_DEV - 1).astype(jnp.int32)
    ghost_slots = with_ends(jax.random.randint(seeds[10], (N_DOM * N_DOM, SEND), 0, BND), jax.random.fold_in(seeds[10], 1), 0, BND - 1).astype(jnp.int32)
    edges_in = draw_edges_in(jax.random.fold_in(seeds[13], 71), 0)
    edges_bd = draw_edges_bd(jax.random.fold_in(seeds[13], 71), 0)
    return {"h_in": h_in, "cotangent": cotangent, "w_one": w_one, "w_two": w_two, "rel_one": rel_one, "rel_two": rel_two, "query_emb": query_emb, "q_head": q_head, "q_rel": q_rel, "bnd_rows": bnd_rows, "ghost_slots": ghost_slots, "edges_in": edges_in, "edges_bd": edges_bd}


def reference(h_in, cotangent, w_one, w_two, rel_one, rel_two, query_emb, q_head, q_rel, bnd_rows, ghost_slots, edges_in, edges_bd):
    block_in = jnp.arange(N_DOM * EIN, dtype=jnp.int32) // EIN
    block_bd = jnp.arange(N_DOM * EBD, dtype=jnp.int32) // EBD
    sources_in = block_in * ENT_DEV + edges_in[0]
    targets_in = block_in * ENT_DEV + edges_in[1]
    ghost_index = edges_bd[0]
    peer_index = ghost_index // SEND
    slot_pos = ghost_index % SEND
    slot_index = ghost_slots[block_bd * N_DOM + peer_index, slot_pos]
    sources_bd = peer_index * ENT_DEV + bnd_rows[peer_index * BND + slot_index]
    targets_bd = block_bd * ENT_DEV + edges_bd[1]
    sources = jnp.concatenate([sources_in, sources_bd]).astype(jnp.int32)
    targets = jnp.concatenate([targets_in, targets_bd]).astype(jnp.int32)
    relations = jnp.concatenate([edges_in[2], edges_bd[2]]).astype(jnp.int32)

    def rel_lookup(rel_table):
        extended = jnp.concatenate([rel_table.astype(jnp.float32), jnp.zeros((1, D), jnp.float32)], axis=0)
        return extended[relations]
    rows_one = rel_lookup(rel_one)
    rows_two = rel_lookup(rel_two)

    def forward(hidden, rel_rows, weight, boost):
        message = hidden[sources].astype(jnp.float32) * rel_rows
        summed = jax.ops.segment_sum(message, targets, num_segments=ENTITIES) + boost
        summed_b = summed.astype(jnp.bfloat16)
        mixed = jnp.dot(summed_b, weight, preferred_element_type=jnp.float32)
        center = mixed - lax.optimization_barrier(jnp.mean(mixed, axis=-1, keepdims=True))
        rstd = lax.rsqrt(lax.optimization_barrier(jnp.mean(center * center, axis=-1, keepdims=True)) + 1e-05)
        return (summed_b, center * rstd, rstd)

    def backward(upstream, hidden, rel_rows, weight, summed_b, normed, rstd):
        sigmoid_val = jax.nn.sigmoid(normed)
        dact = upstream * sigmoid_val * (1.0 + normed * (1.0 - sigmoid_val))
        dmix = rstd * (dact - lax.optimization_barrier(jnp.mean(dact, axis=-1, keepdims=True)) - normed * lax.optimization_barrier(jnp.mean(dact * normed, axis=-1, keepdims=True)))
        dmix_b = dmix.astype(jnp.bfloat16)
        wgrad = jnp.dot(summed_b.T, dmix_b, preferred_element_type=jnp.float32)
        dsum = jnp.dot(dmix_b, weight.T, preferred_element_type=jnp.float32).astype(jnp.bfloat16)
        dmessage = dsum[targets].astype(jnp.float32)
        rgrad = jax.ops.segment_sum(dmessage * hidden[sources].astype(jnp.float32), relations, num_segments=NREL + 1)[:NREL]
        dhidden = upstream + jax.ops.segment_sum(dmessage * rel_rows, sources, num_segments=ENTITIES)
        return (dhidden, wgrad, rgrad)

    def per_query(qnum):
        start = qnum * D
        first = lax.dynamic_slice_in_dim(h_in, start, D, 1)
        cot_part = lax.dynamic_slice_in_dim(cotangent, start, D, 1).astype(jnp.float32)
        boost = jnp.zeros((ENTITIES, D), jnp.float32).at[q_head[qnum]].add(query_emb[q_rel[qnum]].astype(jnp.float32))
        sum_one, norm_one, rstd_one = forward(first, rows_one, w_one, boost)
        second = (jax.nn.silu(norm_one) + first.astype(jnp.float32)).astype(jnp.bfloat16)
        sum_two, norm_two, rstd_two = forward(second, rows_two, w_two, boost)
        grad_mid, wg_two, rg_two = backward(cot_part, second, rows_two, w_two, sum_two, norm_two, rstd_two)
        grad_first, wg_one, rg_one = backward(grad_mid, first, rows_one, w_one, sum_one, norm_one, rstd_one)
        return (grad_first, jnp.stack([wg_one, wg_two]), jnp.stack([rg_one, rg_two]))
    grads_all, wgrads, rgrads = lax.map(per_query, jnp.arange(QUERIES, dtype=jnp.int32))
    grad_in = jnp.transpose(grads_all, (1, 0, 2)).reshape(ENTITIES, QUERIES * D)
    scale_w = 1.0 / jnp.sqrt(jnp.float32(ENTITIES * QUERIES))
    scale_r = jnp.sqrt(jnp.float32(NREL) / jnp.float32(N_DOM * (EIN + EBD) * QUERIES))
    return (grad_in, lax.optimization_barrier(jnp.sum(wgrads, axis=0)) * scale_w, lax.optimization_barrier(jnp.sum(rgrads, axis=0)) * scale_r)
```

```python
import functools
import math

import jax
import jax.numpy as jnp
from jax import lax
from jax.experimental import pallas as pl
from jax.experimental.pallas import tpu as pltpu
from jax.sharding import PartitionSpec as P

MESH = pl.DeviceIdType.MESH
F32 = jnp.float32
BF16 = jnp.bfloat16
RS_EARLY = False


def dot_nn(a, b):
    return lax.dot_general(a, b, (((1,), (0,)), ((), ())), preferred_element_type=F32)


def dot_nt(a, b):
    return lax.dot_general(a, b, (((1,), (1,)), ((), ())), preferred_element_type=F32)


def split_hi_lo(x, axis):
    hi = x.astype(BF16)
    lo = (x - hi.astype(F32)).astype(BF16)
    return jnp.concatenate([hi, lo], axis=axis)


def onehot_into(dest, ids, col0, block):
    rows = dest.shape[0]
    count = ids.shape[1]

    def fill(i, carry):
        base = pl.multiple_of(i * block, block)
        row_ids = lax.broadcasted_iota(jnp.int32, (block, count), 0) + base
        dest[pl.ds(base, block), pl.ds(col0, count)] = jnp.where(row_ids == ids, 1.0, 0.0).astype(BF16)
        return carry

    lax.fori_loop(0, rows // block, fill, 0)


def loop(low, high, step):
    if high - low <= 32:
        for i in range(low, high):
            step(i, 0)
    else:
        lax.fori_loop(low, high, step, 0)


def div(a, b):
    return a // b if isinstance(a, int) else lax.div(a, b)


def rem(a, b):
    return a % b if isinstance(a, int) else lax.rem(a, b)


def aligned(a, b):
    return a if isinstance(a, int) else pl.multiple_of(a, b)


def kernel(
    n_q,
    n_d,
    grp,
    scale_w,
    scale_r,
    rel_count,
    rel_rows,
    *refs,
):
    n_in = 13
    hbm = refs[:n_in]
    gin_ref, gw_ref, grel_ref = refs[n_in : n_in + 3]
    local = refs[n_in + 3 : 2 * n_in + 3]
    (
        h_ref, cot_ref, w1_ref, w2_ref, r1_ref, r2_ref, qe_ref, qhead_ref, qrel_ref, bnd_ref, gs_ref, ein_ref, ebd_ref,
    ) = local
    (
    relt,
    gs_x,
    rt,
    vt,
    st_in,
    st_bd,
    rel_e,
    x1,
    x2,
    req,
    out1,
    ghost1,
    out2,
    ghost2,
    ret_out2,
    ret_in2,
    ret_out1,
    ret_in1,
    red_src,
    red_in,
    red_z,
    red_all,
    xsend,
    xrecv,
    asend,
    arecv,
    load_sem,
    ) = refs[2 * n_in + 3 :]
    me_d = lax.axis_index("dom")
    me_q = lax.axis_index("query")
    n_far = n_d // grp
    n_near = n_q * grp
    far = lax.div(me_d, grp)
    near = lax.rem(me_d, grp)
    me_n = me_q * grp + near
    feat = w1_ref.shape[0]
    rows, wide = h_ref.shape
    queries = wide // feat
    send = ghost1.shape[0] // n_d
    e_in = ein_ref.shape[1]
    e_bd = ebd_ref.shape[1]
    width = red_src.shape[3]

    barrier = pltpu.get_barrier_semaphore()

    def greet(i, carry):
        t = lax.rem(me_d + i, n_d)
        pl.semaphore_signal(barrier, inc=1, device_id=(me_q, t), device_id_type=MESH)
        return carry

    loop(1, n_d, greet)
    for dq in range(1, n_q):
        for k in range(grp):
            pl.semaphore_signal(
                barrier,
                inc=1,
                device_id=(lax.rem(me_q + dq, n_q), far * grp + k),
                device_id_type=MESH,
            )
    greeted = n_d - 1 + (n_q - 1) * grp
    loads = [
        pltpu.make_async_copy(src, dst, load_sem.at[k])
        for k, (src, dst) in enumerate(zip(hbm, local))
    ]
    for load in loads[::-1]:
        load.start()
    for load in loads[::-1]:
        load.wait()

    def peer_loop(step):
        if n_d <= 32:
            order = sorted(range(1, n_d), key=lambda i: -min(i // grp, n_far - i // grp))
            for i in order:
                step(i, 0)
        else:
            lax.fori_loop(1, n_d, step, 0)

    def exchange_start(phase, src, dst, size):
        def go(i, carry):
            peer = lax.rem(me_d + i, n_d)
            if size is None:
                s, d = src.at[peer], dst.at[me_d]
            else:
                s = src.at[pl.ds(pl.multiple_of(peer * size, size), size)]
                d = dst.at[pl.ds(pl.multiple_of(me_d * size, size), size)]
            pltpu.make_async_remote_copy(
                src_ref=s,
                dst_ref=d,
                send_sem=xsend.at[phase],
                recv_sem=xrecv.at[phase],
                device_id=(me_q, peer),
                device_id_type=MESH,
            ).start()
            return carry

        peer_loop(go)
        if size is None:
            dst[me_d] = src[me_d]
        else:
            own = pl.ds(pl.multiple_of(me_d * size, size), size)
            dst[own, :] = src[own, :]

    def exchange_wait(phase, src, dst, size):
        some = pl.ds(0, (n_d - 1) * (size or 1))
        pltpu.make_async_remote_copy(
            src_ref=src.at[some],
            dst_ref=dst.at[some],
            send_sem=xsend.at[phase],
            recv_sem=xrecv.at[phase],
            device_id=(me_q, lax.rem(me_d + 1, n_d)),
            device_id_type=MESH,
        ).wait()

    def near_device(t):
        return lax.div(t, grp), far * grp + lax.rem(t, grp)

    def all_copy(layer, stage, src, dst, device):
        return pltpu.make_async_remote_copy(
            src_ref=src,
            dst_ref=dst,
            send_sem=asend.at[layer, stage],
            recv_sem=arecv.at[layer, stage],
            device_id=device,
            device_id_type=MESH,
        )

    def scatter_start(layer):
        def go(j, carry):
            t = lax.rem(me_n + j, n_near)
            all_copy(layer, 0, red_src.at[layer, t], red_in.at[layer, me_n], near_device(t)).start()
            return carry

        loop(1, n_near, go)

    def far_start(layer):
        some = pl.ds(0, n_near - 1)
        all_copy(
            layer, 0, red_src.at[layer, some], red_in.at[layer, some], near_device(lax.rem(me_n + 1, n_near))
        ).wait()
        red_in[layer, me_n] = red_src[layer, me_n]
        red_z[layer, far] = jnp.sum(red_in[layer].astype(F32), axis=0).astype(BF16)

        def go(j, carry):
            t = lax.rem(far + j, n_far)
            all_copy(layer, 1, red_z.at[layer, far], red_z.at[layer, far], (me_q, t * grp + near)).start()
            return carry

        loop(1, n_far, go)

    def gather_start(layer):
        if n_far > 1:
            some = pl.ds(0, n_far - 1)
            all_copy(
                layer,
                1,
                red_z.at[layer, some],
                red_z.at[layer, some],
                (me_q, lax.rem(far + 1, n_far) * grp + near),
            ).wait()
        red_all[layer, me_n] = jnp.sum(red_z[layer].astype(F32), axis=0).astype(BF16)

        def go(j, carry):
            t = lax.rem(me_n + j, n_near)
            all_copy(layer, 2, red_all.at[layer, me_n], red_all.at[layer, me_n], near_device(t)).start()
            return carry

        loop(1, n_near, go)

    def gather_wait(layer):
        some = pl.ds(0, n_near - 1)
        all_copy(
            layer, 2, red_all.at[layer, some], red_all.at[layer, some], near_device(lax.rem(me_n + 1, n_near))
        ).wait()

    def pack(layer, rg, wg):
        parts = [rg, wg]
        left = width - rel_rows - feat
        if left:
            parts.append(jnp.zeros((feat, left), F32))
        whole = jnp.concatenate(parts, axis=1)
        red_src[layer] = whole.reshape(n_near, feat // n_near, width).astype(BF16)

    def unpack(layer):
        summed = red_all[layer].astype(F32).reshape(feat, width)
        grel_ref[layer] = summed[:, :rel_count] * scale_r
        gw_ref[layer] = summed[:, rel_rows : rel_rows + feat] * scale_w

    per = 128 // send
    spread = jnp.concatenate([gs_ref[...]] * per, axis=1)
    for p in range(n_d):
        gs_x[p] = spread[p : p + 1, :]

    onehot_into(vt, ein_ref[1:2, :], 0, 64)
    onehot_into(vt, ebd_ref[1:2, :], e_in, 64)
    pl.semaphore_wait(barrier, greeted)
    exchange_start(0, gs_x, req, None)
    onehot_into(st_in, ein_ref[0:1, :], 0, 64)
    onehot_into(st_bd, ebd_ref[0:1, :], 0, 64)

    slots = bnd_ref.shape[1]
    own_ids = lax.broadcasted_iota(jnp.int32, (rows, slots), 0)
    row_of32 = jnp.where(own_ids == bnd_ref[...], 1.0, 0.0)
    row_of = row_of32.astype(BF16)
    published = dot_nn(row_of32.T.astype(BF16), h_ref[...]).astype(BF16)

    exchange_wait(0, gs_x, req, None)
    lane_group = lax.broadcasted_iota(jnp.int32, (1, 128), 1) // send
    wanted = []
    for j in range(n_d // per):
        vec = jnp.zeros((1, 128), jnp.int32)
        for k in range(per):
            vec = jnp.where(lane_group == k, req[j * per + k, 0:1, :], vec)
        wanted.append(vec)
    wanted = jnp.concatenate(wanted, axis=1)
    slot_ids = lax.broadcasted_iota(jnp.int32, (slots, n_d * send), 0)
    slot_of32 = jnp.where(slot_ids == wanted, 1.0, 0.0)
    slot_of_t = slot_of32.T.astype(BF16)
    out1[...] = dot_nn(slot_of_t, published).astype(BF16)
    exchange_start(1, out1, ghost1, send)

    onehot_into(rt, ein_ref[2:3, :], 0, 32)
    onehot_into(rt, ebd_ref[2:3, :], e_in, 32)
    relt[...] = jnp.zeros_like(relt)
    relt[pl.ds(0, feat), pl.ds(0, rel_count)] = r1_ref[...]
    relt[pl.ds(feat, feat), pl.ds(0, rel_count)] = r2_ref[...]
    rel_e[...] = dot_nn(relt[...], rt[...]).astype(BF16)
    pick_t = dot_nn(row_of, slot_of32.astype(BF16)).astype(BF16)
    pick = dot_nt(slot_of_t, row_of).astype(BF16)

    row_ids = lax.broadcasted_iota(jnp.int32, (feat, rows), 1) + me_d * rows
    lane_rel = lax.broadcasted_iota(jnp.int32, (feat, rel_count), 1)
    qtab = qe_ref[...].astype(F32)
    boost_parts = []
    for q in range(queries):
        vec = jnp.sum(jnp.where(lane_rel == qrel_ref[q], qtab, 0.0), axis=1, keepdims=True)
        boost_parts.append(jnp.where(row_ids == qhead_ref[q], vec, 0.0))
    boost = jnp.concatenate(boost_parts, axis=0)

    h32 = h_ref[...].astype(F32)
    h_t32 = h32.T
    h_t = h_t32.astype(BF16)

    def rel_tile(layer, lo, count):
        part = rel_e[pl.ds(layer * feat, feat), pl.ds(lo, count)].astype(F32)
        return jnp.concatenate([part] * queries, axis=0)

    def aggregate(layer, table_t, onehot, save, lo, count):
        sourced = dot_nn(table_t, onehot[...])
        save[:, pl.ds(lo, count)] = sourced.astype(BF16)
        message = split_hi_lo(sourced * rel_tile(layer, lo, count), 0)
        both = dot_nt(message, vt[:, pl.ds(lo, count)])
        return both[:wide] + both[wide:]

    def normalise(summed, w_ref):
        summed_b = summed.astype(BF16)
        normed, rstds = [], []
        for q in range(queries):
            mixed = lax.dot_general(
                w_ref[...],
                summed_b[q * feat : (q + 1) * feat],
                (((0,), (0,)), ((), ())),
                preferred_element_type=F32,
            )
            center = mixed - jnp.mean(mixed, axis=0, keepdims=True)
            rstd = lax.rsqrt(jnp.mean(center * center, axis=0, keepdims=True) + 1e-05)
            normed.append(center * rstd)
            rstds.append(rstd)
        return summed_b, normed, rstds

    def back_layer(up_t, normed, rstds, summed_b, w_ref):
        wgrad = jnp.zeros((feat, feat), F32)
        dsum = []
        for q in range(queries):
            y = normed[q]
            sig = jax.nn.sigmoid(y)
            dact = up_t[q * feat : (q + 1) * feat] * sig * (1.0 + y * (1.0 - sig))
            dmix = rstds[q] * (
                dact
                - jnp.mean(dact, axis=0, keepdims=True)
                - y * jnp.mean(dact * y, axis=0, keepdims=True)
            )
            dmix_b = dmix.astype(BF16)
            wgrad = wgrad + dot_nt(summed_b[q * feat : (q + 1) * feat], dmix_b)
            dsum.append(dot_nn(w_ref[...], dmix_b).astype(BF16))
        return wgrad, jnp.concatenate(dsum, axis=0)

    def rel_grad(downs, save):
        tots = []
        lo = 0
        for down in downs:
            count = down.shape[1]
            prod = down * save[:, pl.ds(lo, count)].astype(F32)
            tot = prod[:feat]
            for q in range(1, queries):
                tot = tot + prod[q * feat : (q + 1) * feat]
            tots.append(split_hi_lo(tot, 0))
            lo += count
        both = dot_nt(jnp.concatenate(tots, axis=1), rt[pl.ds(0, rel_rows), :])
        return both[:feat] + both[feat:]

    def table_grad(layer, down, onehot, lo, count):
        message = split_hi_lo(down * rel_tile(layer, lo, count), 0)
        both = dot_nt(onehot[...], message)
        return both[:, :wide] + both[:, wide:]

    def give_back(ret_in):
        return dot_nn(pick_t, ret_in[...])

    sum1 = aggregate(0, h_t, st_in, x1, 0, e_in) + boost
    exchange_wait(1, out1, ghost1, send)
    sum1 = sum1 + aggregate(0, ghost1[...].astype(F32).T.astype(BF16), st_bd, x1, e_in, e_bd)
    sum1_b, norm1, rstd1 = normalise(sum1, w1_ref)
    h2_t = (
        jnp.concatenate([y * jax.nn.sigmoid(y) for y in norm1], axis=0) + h_t32
    ).astype(BF16)

    out2[...] = dot_nt(pick, h2_t).astype(BF16)
    exchange_start(2, out2, ghost2, send)
    sum2 = aggregate(1, h2_t, st_in, x2, 0, e_in) + boost
    exchange_wait(2, out2, ghost2, send)
    sum2 = sum2 + aggregate(1, ghost2[...].astype(F32).T.astype(BF16), st_bd, x2, e_in, e_bd)
    sum2_b, norm2, rstd2 = normalise(sum2, w2_ref)

    cot32 = cot_ref[...].astype(F32)
    wg2, dsum2 = back_layer(cot32.T, norm2, rstd2, sum2_b, w2_ref)
    down2_bd = dot_nn(dsum2, vt[:, pl.ds(e_in, e_bd)])
    ret_out2[...] = table_grad(1, down2_bd, st_bd, e_in, e_bd).astype(BF16)
    exchange_start(3, ret_out2, ret_in2, send)
    down2_in = dot_nn(dsum2, vt[:, pl.ds(0, e_in)])
    mid = cot32 + table_grad(1, down2_in, st_in, 0, e_in)
    pack(1, rel_grad((down2_in, down2_bd), x2), wg2)
    if RS_EARLY:
        scatter_start(1)
    exchange_wait(3, ret_out2, ret_in2, send)
    if not RS_EARLY:
        scatter_start(1)
    mid = mid + give_back(ret_in2)

    wg1, dsum1 = back_layer(mid.T, norm1, rstd1, sum1_b, w1_ref)
    down1_in = dot_nn(dsum1, vt[:, pl.ds(0, e_in)])
    down1_bd = dot_nn(dsum1, vt[:, pl.ds(e_in, e_bd)])
    pack(0, rel_grad((down1_in, down1_bd), x1), wg1)
    scatter_start(0)
    far_start(1)
    ret_out1[...] = table_grad(0, down1_bd, st_bd, e_in, e_bd).astype(BF16)
    exchange_start(4, ret_out1, ret_in1, send)
    base = mid + table_grad(0, down1_in, st_in, 0, e_in)
    far_start(0)
    gather_start(1)
    exchange_wait(4, ret_out1, ret_in1, send)
    gin_ref[...] = base + give_back(ret_in1)
    gather_start(0)
    gather_wait(1)
    unpack(1)
    gather_wait(0)
    unpack(0)


def write_out(*refs):
    half = (len(refs) - 1) // 2
    copies = [
        pltpu.make_async_copy(src, dst, refs[-1].at[k])
        for k, (src, dst) in enumerate(zip(refs[:half], refs[half : 2 * half]))
    ]
    for copy in copies:
        copy.start()
    for copy in copies:
        copy.wait()


def body(
    h_in,
    cotangent,
    w_one,
    w_two,
    rel_one,
    rel_two,
    query_emb,
    q_head,
    q_rel,
    bnd_rows,
    ghost_slots,
    edges_in,
    edges_bd,
):
    rows, wide = h_in.shape
    feat = w_one.shape[0]
    queries = wide // feat
    rel_count = rel_one.shape[0]
    n_d = lax.axis_size("dom")
    n_q = lax.axis_size("query")
    send = ghost_slots.shape[1]
    ghosts = n_d * send
    e_in, e_bd = edges_in.shape[1], edges_bd.shape[1]
    edges = e_in + e_bd
    rel_pad = -(-(rel_count + 1) // 128) * 128
    rel_rows = -(-(rel_count + 1) // 16) * 16
    width = -(-(rel_rows + feat) // 128) * 128
    grp = max(1, 8 // n_q)
    n_near, n_far = n_q * grp, n_d // grp
    part = feat // n_near
    scale_w = 1.0 / math.sqrt(rows * n_d * queries * n_q)
    scale_r = math.sqrt(rel_count / (n_d * edges * queries * n_q))

    args = (
        h_in,
        cotangent,
        w_one,
        w_two,
        rel_one.T,
        rel_two.T,
        query_emb.T,
        q_head,
        q_rel,
        bnd_rows[None, :],
        ghost_slots,
        edges_in,
        edges_bd,
    )
    spaces = [pltpu.VMEM] * 7 + [pltpu.SMEM] * 2 + [pltpu.VMEM] * 4

    vmem = pl.BlockSpec(memory_space=pltpu.VMEM)
    dma = pltpu.SemaphoreType.DMA
    shapes = (
        jax.ShapeDtypeStruct((rows, wide), F32),
        jax.ShapeDtypeStruct((2, feat, feat), F32),
        jax.ShapeDtypeStruct((2, feat, rel_count), F32),
    )
    results = pl.pallas_call(
        functools.partial(kernel, n_q, n_d, grp, scale_w, scale_r, rel_count, rel_rows),
        out_shape=shapes,
        in_specs=[pl.BlockSpec(memory_space=pltpu.HBM)] * len(args),
        out_specs=(vmem, vmem, vmem),
        scratch_shapes=[
            *(space(a.shape, a.dtype) for a, space in zip(args, spaces)),
            pltpu.VMEM((2 * feat, rel_pad), BF16),
            pltpu.VMEM((n_d, 1, 128), jnp.int32),
            pltpu.VMEM((rel_pad, edges), BF16),
            pltpu.VMEM((rows, edges), BF16),
            pltpu.VMEM((rows, e_in), BF16),
            pltpu.VMEM((ghosts, e_bd), BF16),
            pltpu.VMEM((2 * feat, edges), BF16),
            pltpu.VMEM((wide, edges), BF16),
            pltpu.VMEM((wide, edges), BF16),
            pltpu.VMEM((n_d, 1, 128), jnp.int32),
            pltpu.VMEM((ghosts, wide), BF16),
            pltpu.VMEM((ghosts, wide), BF16),
            pltpu.VMEM((ghosts, wide), BF16),
            pltpu.VMEM((ghosts, wide), BF16),
            pltpu.VMEM((ghosts, wide), BF16),
            pltpu.VMEM((ghosts, wide), BF16),
            pltpu.VMEM((ghosts, wide), BF16),
            pltpu.VMEM((ghosts, wide), BF16),
            pltpu.VMEM((2, n_near, part, width), BF16),
            pltpu.VMEM((2, n_near, part, width), BF16),
            pltpu.VMEM((2, n_far, part, width), BF16),
            pltpu.VMEM((2, n_near, part, width), BF16),
            dma((5,)),
            dma((5,)),
            dma((2, 3)),
            dma((2, 3)),
            dma((len(args),)),
        ],
        compiler_params=pltpu.CompilerParams(
            collective_id=0, has_side_effects=True, vmem_limit_bytes=33554432
        ),
    )(*args)
    grad_in, grad_w, grad_rel_t = pl.pallas_call(
        write_out,
        out_shape=shapes,
        in_specs=[vmem] * 3,
        out_specs=[pl.BlockSpec(memory_space=pltpu.HBM)] * 3,
        scratch_shapes=[dma((3,))],
    )(*results)
    return grad_in, grad_w, jnp.swapaxes(grad_rel_t, 1, 2)


def solution(mesh):
    return jax.shard_map(
        body,
        mesh=mesh,
        in_specs=(
            P("dom", "query"),
            P("dom", "query"),
            P(),
            P(),
            P(),
            P(),
            P(),
            P("query"),
            P("query"),
            P("dom"),
            P("dom", None),
            P(None, "dom"),
            P(None, "dom"),
        ),
        out_specs=(P("dom", "query"), P(), P()),
        check_vma=False,
    )
```

```python
import functools
import math

import jax
import jax.numpy as jnp
from jax import lax
from jax.experimental import pallas as pl
from jax.experimental.pallas import tpu as pltpu
from jax.sharding import PartitionSpec as P

MESH = pl.DeviceIdType.MESH
F32 = jnp.float32
BF16 = jnp.bfloat16
RS_EARLY = False


def dot_nn(a, b):
    return lax.dot_general(a, b, (((1,), (0,)), ((), ())), preferred_element_type=F32)


def dot_nt(a, b):
    return lax.dot_general(a, b, (((1,), (1,)), ((), ())), preferred_element_type=F32)


def split_hi_lo(x, axis):
    hi = x.astype(BF16)
    lo = (x - hi.astype(F32)).astype(BF16)
    return jnp.concatenate([hi, lo], axis=axis)


def onehot_into(dest, ids, col0, block):
    rows = dest.shape[0]
    count = ids.shape[1]

    def fill(i, carry):
        base = pl.multiple_of(i * block, block)
        row_ids = lax.broadcasted_iota(jnp.int32, (block, count), 0) + base
        dest[pl.ds(base, block), pl.ds(col0, count)] = jnp.where(row_ids == ids, 1.0, 0.0).astype(BF16)
        return carry

    lax.fori_loop(0, rows // block, fill, 0)


def loop(low, high, step):
    if high - low <= 32:
        for i in range(low, high):
            step(i, 0)
    else:
        lax.fori_loop(low, high, step, 0)


def div(a, b):
    return a // b if isinstance(a, int) else lax.div(a, b)


def rem(a, b):
    return a % b if isinstance(a, int) else lax.rem(a, b)


def aligned(a, b):
    return a if isinstance(a, int) else pl.multiple_of(a, b)


def kernel(
    n_q,
    n_d,
    grp,
    scale_w,
    scale_r,
    rel_count,
    rel_rows,
    *refs,
):
    n_in = 13
    hbm = refs[:n_in]
    gin_ref, gw_ref, grel_ref = refs[n_in : n_in + 3]
    local = refs[n_in + 3 : 2 * n_in + 3]
    (
        h_ref, cot_ref, w1_ref, w2_ref, r1_ref, r2_ref, qe_ref, qhead_ref, qrel_ref, bnd_ref, gs_ref, ein_ref, ebd_ref,
    ) = local
    (
    relt,
    gs_x,
    rt,
    vt,
    st_in,
    st_bd,
    rel_e,
    x1,
    x2,
    req,
    out1,
    ghost1,
    out2,
    ghost2,
    ret_out2,
    ret_in2,
    ret_out1,
    ret_in1,
    red_src,
    red_in,
    red_z,
    red_all,
    xsend,
    xrecv,
    asend,
    arecv,
    load_sem,
    ) = refs[2 * n_in + 3 :]
    me_d = lax.axis_index("dom")
    me_q = lax.axis_index("query")
    n_far = n_d // grp
    n_near = n_q * grp
    far = lax.div(me_d, grp)
    near = lax.rem(me_d, grp)
    me_n = me_q * grp + near
    feat = w1_ref.shape[0]
    rows, wide = h_ref.shape
    queries = wide // feat
    send = ghost1.shape[0] // n_d
    e_in = ein_ref.shape[1]
    e_bd = ebd_ref.shape[1]
    width = red_src.shape[3]

    barrier = pltpu.get_barrier_semaphore()

    def greet(i, carry):
        t = lax.rem(me_d + i, n_d)
        pl.semaphore_signal(barrier, inc=1, device_id=(me_q, t), device_id_type=MESH)
        return carry

    loop(1, n_d, greet)
    for dq in range(1, n_q):
        for k in range(grp):
            pl.semaphore_signal(
                barrier,
                inc=1,
                device_id=(lax.rem(me_q + dq, n_q), far * grp + k),
                device_id_type=MESH,
            )
    greeted = n_d - 1 + (n_q - 1) * grp
    loads = [
        pltpu.make_async_copy(src, dst, load_sem.at[k])
        for k, (src, dst) in enumerate(zip(hbm, local))
    ]
    for load in loads[::-1]:
        load.start()
    for load in loads[::-1]:
        load.wait()

    def peer_loop(step):
        if n_d <= 32:
            order = sorted(range(1, n_d), key=lambda i: -min(i // grp, n_far - i // grp))
            for i in order:
                step(i, 0)
        else:
            lax.fori_loop(1, n_d, step, 0)

    def exchange_start(phase, src, dst, size):
        def go(i, carry):
            peer = lax.rem(me_d + i, n_d)
            if size is None:
                s, d = src.at[peer], dst.at[me_d]
            else:
                s = src.at[pl.ds(pl.multiple_of(peer * size, size), size)]
                d = dst.at[pl.ds(pl.multiple_of(me_d * size, size), size)]
            pltpu.make_async_remote_copy(
                src_ref=s,
                dst_ref=d,
                send_sem=xsend.at[phase],
                recv_sem=xrecv.at[phase],
                device_id=(me_q, peer),
                device_id_type=MESH,
            ).start()
            return carry

        peer_loop(go)
        if size is None:
            dst[me_d] = src[me_d]
        else:
            own = pl.ds(pl.multiple_of(me_d * size, size), size)
            dst[own, :] = src[own, :]

    def exchange_wait(phase, src, dst, size):
        some = pl.ds(0, (n_d - 1) * (size or 1))
        pltpu.make_async_remote_copy(
            src_ref=src.at[some],
            dst_ref=dst.at[some],
            send_sem=xsend.at[phase],
            recv_sem=xrecv.at[phase],
            device_id=(me_q, lax.rem(me_d + 1, n_d)),
            device_id_type=MESH,
        ).wait()

    def near_device(t):
        return lax.div(t, grp), far * grp + lax.rem(t, grp)

    def all_copy(layer, stage, src, dst, device):
        return pltpu.make_async_remote_copy(
            src_ref=src,
            dst_ref=dst,
            send_sem=asend.at[layer, stage],
            recv_sem=arecv.at[layer, stage],
            device_id=device,
            device_id_type=MESH,
        )

    def scatter_start(layer):
        def go(j, carry):
            t = lax.rem(me_n + j, n_near)
            all_copy(layer, 0, red_src.at[layer, t], red_in.at[layer, me_n], near_device(t)).start()
            return carry

        loop(1, n_near, go)

    def far_start(layer):
        some = pl.ds(0, n_near - 1)
        all_copy(
            layer, 0, red_src.at[layer, some], red_in.at[layer, some], near_device(lax.rem(me_n + 1, n_near))
        ).wait()
        red_in[layer, me_n] = red_src[layer, me_n]
        red_z[layer, far] = jnp.sum(red_in[layer].astype(F32), axis=0).astype(BF16)

        def go(j, carry):
            t = lax.rem(far + j, n_far)
            all_copy(layer, 1, red_z.at[layer, far], red_z.at[layer, far], (me_q, t * grp + near)).start()
            return carry

        loop(1, n_far, go)

    def gather_start(layer):
        if n_far > 1:
            some = pl.ds(0, n_far - 1)
            all_copy(
                layer,
                1,
                red_z.at[layer, some],
                red_z.at[layer, some],
                (me_q, lax.rem(far + 1, n_far) * grp + near),
            ).wait()
        red_all[layer, me_n] = jnp.sum(red_z[layer].astype(F32), axis=0).astype(BF16)

        def go(j, carry):
            t = lax.rem(me_n + j, n_near)
            all_copy(layer, 2, red_all.at[layer, me_n], red_all.at[layer, me_n], near_device(t)).start()
            return carry

        loop(1, n_near, go)

    def gather_wait(layer):
        some = pl.ds(0, n_near - 1)
        all_copy(
            layer, 2, red_all.at[layer, some], red_all.at[layer, some], near_device(lax.rem(me_n + 1, n_near))
        ).wait()

    def pack(layer, rg, wg):
        parts = [rg, wg]
        left = width - rel_rows - feat
        if left:
            parts.append(jnp.zeros((feat, left), F32))
        whole = jnp.concatenate(parts, axis=1)
        red_src[layer] = whole.reshape(n_near, feat // n_near, width).astype(BF16)

    def unpack(layer):
        summed = red_all[layer].astype(F32).reshape(feat, width)
        grel_ref[layer] = summed[:, :rel_count] * scale_r
        gw_ref[layer] = summed[:, rel_rows : rel_rows + feat] * scale_w

    per = 128 // send
    spread = jnp.concatenate([gs_ref[...]] * per, axis=1)
    for p in range(n_d):
        gs_x[p] = spread[p : p + 1, :]

    onehot_into(vt, ein_ref[1:2, :], 0, 64)
    onehot_into(vt, ebd_ref[1:2, :], e_in, 64)
    pl.semaphore_wait(barrier, greeted)
    exchange_start(0, gs_x, req, None)
    onehot_into(st_in, ein_ref[0:1, :], 0, 64)
    onehot_into(st_bd, ebd_ref[0:1, :], 0, 64)

    slots = bnd_ref.shape[1]
    own_ids = lax.broadcasted_iota(jnp.int32, (rows, slots), 0)
    row_of32 = jnp.where(own_ids == bnd_ref[...], 1.0, 0.0)
    row_of = row_of32.astype(BF16)
    published = dot_nn(row_of32.T.astype(BF16), h_ref[...]).astype(BF16)

    exchange_wait(0, gs_x, req, None)
    lane_group = lax.broadcasted_iota(jnp.int32, (1, 128), 1) // send
    wanted = []
    for j in range(n_d // per):
        vec = jnp.zeros((1, 128), jnp.int32)
        for k in range(per):
            vec = jnp.where(lane_group == k, req[j * per + k, 0:1, :], vec)
        wanted.append(vec)
    wanted = jnp.concatenate(wanted, axis=1)
    slot_ids = lax.broadcasted_iota(jnp.int32, (slots, n_d * send), 0)
    slot_of32 = jnp.where(slot_ids == wanted, 1.0, 0.0)
    slot_of_t = slot_of32.T.astype(BF16)
    out1[...] = dot_nn(slot_of_t, published).astype(BF16)
    exchange_start(1, out1, ghost1, send)

    onehot_into(rt, ein_ref[2:3, :], 0, 32)
    onehot_into(rt, ebd_ref[2:3, :], e_in, 32)
    relt[...] = jnp.zeros_like(relt)
    relt[pl.ds(0, feat), pl.ds(0, rel_count)] = r1_ref[...]
    relt[pl.ds(feat, feat), pl.ds(0, rel_count)] = r2_ref[...]
    rel_e[...] = dot_nn(relt[...], rt[...]).astype(BF16)
    pick_t = dot_nn(row_of, slot_of32.astype(BF16)).astype(BF16)
    pick = dot_nt(slot_of_t, row_of).astype(BF16)

    row_ids = lax.broadcasted_iota(jnp.int32, (feat, rows), 1) + me_d * rows
    lane_rel = lax.broadcasted_iota(jnp.int32, (feat, rel_count), 1)
    qtab = qe_ref[...].astype(F32)
    boost_parts = []
    for q in range(queries):
        vec = jnp.sum(jnp.where(lane_rel == qrel_ref[q], qtab, 0.0), axis=1, keepdims=True)
        boost_parts.append(jnp.where(row_ids == qhead_ref[q], vec, 0.0))
    boost = jnp.concatenate(boost_parts, axis=0)

    h32 = h_ref[...].astype(F32)
    h_t32 = h32.T
    h_t = h_t32.astype(BF16)

    def rel_tile(layer, lo, count):
        part = rel_e[pl.ds(layer * feat, feat), pl.ds(lo, count)].astype(F32)
        return jnp.concatenate([part] * queries, axis=0)

    def aggregate(layer, table_t, onehot, save, lo, count):
        sourced = dot_nn(table_t, onehot[...])
        save[:, pl.ds(lo, count)] = sourced.astype(BF16)
        message = split_hi_lo(sourced * rel_tile(layer, lo, count), 0)
        both = dot_nt(message, vt[:, pl.ds(lo, count)])
        return both[:wide] + both[wide:]

    def normalise(summed, w_ref):
        summed_b = summed.astype(BF16)
        normed, rstds = [], []
        for q in range(queries):
            mixed = lax.dot_general(
                w_ref[...],
                summed_b[q * feat : (q + 1) * feat],
                (((0,), (0,)), ((), ())),
                preferred_element_type=F32,
            )
            center = mixed - jnp.mean(mixed, axis=0, keepdims=True)
            rstd = lax.rsqrt(jnp.mean(center * center, axis=0, keepdims=True) + 1e-05)
            normed.append(center * rstd)
            rstds.append(rstd)
        return summed_b, normed, rstds

    def back_layer(up_t, normed, rstds, summed_b, w_ref):
        wgrad = jnp.zeros((feat, feat), F32)
        dsum = []
        for q in range(queries):
            y = normed[q]
            sig = jax.nn.sigmoid(y)
            dact = up_t[q * feat : (q + 1) * feat] * sig * (1.0 + y * (1.0 - sig))
            dmix = rstds[q] * (
                dact
                - jnp.mean(dact, axis=0, keepdims=True)
                - y * jnp.mean(dact * y, axis=0, keepdims=True)
            )
            dmix_b = dmix.astype(BF16)
            wgrad = wgrad + dot_nt(summed_b[q * feat : (q + 1) * feat], dmix_b)
            dsum.append(dot_nn(w_ref[...], dmix_b).astype(BF16))
        return wgrad, jnp.concatenate(dsum, axis=0)

    def rel_grad(downs, save):
        tots = []
        lo = 0
        for down in downs:
            count = down.shape[1]
            prod = down * save[:, pl.ds(lo, count)].astype(F32)
            tot = prod[:feat]
            for q in range(1, queries):
                tot = tot + prod[q * feat : (q + 1) * feat]
            tots.append(split_hi_lo(tot, 0))
            lo += count
        both = dot_nt(jnp.concatenate(tots, axis=1), rt[pl.ds(0, rel_rows), :])
        return both[:feat] + both[feat:]

    def table_grad(layer, down, onehot, lo, count):
        message = split_hi_lo(down * rel_tile(layer, lo, count), 0)
        both = dot_nt(onehot[...], message)
        return both[:, :wide] + both[:, wide:]

    def give_back(ret_in):
        return dot_nn(pick_t, ret_in[...])

    sum1 = aggregate(0, h_t, st_in, x1, 0, e_in) + boost
    exchange_wait(1, out1, ghost1, send)
    sum1 = sum1 + aggregate(0, ghost1[...].astype(F32).T.astype(BF16), st_bd, x1, e_in, e_bd)
    sum1_b, norm1, rstd1 = normalise(sum1, w1_ref)
    h2_t = (
        jnp.concatenate([y * jax.nn.sigmoid(y) for y in norm1], axis=0) + h_t32
    ).astype(BF16)

    out2[...] = dot_nt(pick, h2_t).astype(BF16)
    exchange_start(2, out2, ghost2, send)
    sum2 = aggregate(1, h2_t, st_in, x2, 0, e_in) + boost
    exchange_wait(2, out2, ghost2, send)
    sum2 = sum2 + aggregate(1, ghost2[...].astype(F32).T.astype(BF16), st_bd, x2, e_in, e_bd)
    sum2_b, norm2, rstd2 = normalise(sum2, w2_ref)

    cot32 = cot_ref[...].astype(F32)
    wg2, dsum2 = back_layer(cot32.T, norm2, rstd2, sum2_b, w2_ref)
    down2_bd = dot_nn(dsum2, vt[:, pl.ds(e_in, e_bd)])
    ret_out2[...] = table_grad(1, down2_bd, st_bd, e_in, e_bd).astype(BF16)
    exchange_start(3, ret_out2, ret_in2, send)
    down2_in = dot_nn(dsum2, vt[:, pl.ds(0, e_in)])
    mid = cot32 + table_grad(1, down2_in, st_in, 0, e_in)
    pack(1, rel_grad((down2_in, down2_bd), x2), wg2)
    if RS_EARLY:
        scatter_start(1)
    exchange_wait(3, ret_out2, ret_in2, send)
    if not RS_EARLY:
        scatter_start(1)
    mid = mid + give_back(ret_in2)

    wg1, dsum1 = back_layer(mid.T, norm1, rstd1, sum1_b, w1_ref)
    down1_in = dot_nn(dsum1, vt[:, pl.ds(0, e_in)])
    down1_bd = dot_nn(dsum1, vt[:, pl.ds(e_in, e_bd)])
    pack(0, rel_grad((down1_in, down1_bd), x1), wg1)
    scatter_start(0)
    far_start(1)
    ret_out1[...] = table_grad(0, down1_bd, st_bd, e_in, e_bd).astype(BF16)
    exchange_start(4, ret_out1, ret_in1, send)
    base = mid + table_grad(0, down1_in, st_in, 0, e_in)
    far_start(0)
    gather_start(1)
    exchange_wait(4, ret_out1, ret_in1, send)
    gin_ref[...] = base + give_back(ret_in1)
    gather_start(0)
    gather_wait(1)
    unpack(1)
    gather_wait(0)
    unpack(0)


def write_out(*refs):
    half = (len(refs) - 1) // 2
    copies = [
        pltpu.make_async_copy(src, dst, refs[-1].at[k])
        for k, (src, dst) in enumerate(zip(refs[:half], refs[half : 2 * half]))
    ]
    for copy in copies:
        copy.start()
    for copy in copies:
        copy.wait()


def body(
    h_in,
    cotangent,
    w_one,
    w_two,
    rel_one,
    rel_two,
    query_emb,
    q_head,
    q_rel,
    bnd_rows,
    ghost_slots,
    edges_in,
    edges_bd,
):
    rows, wide = h_in.shape
    feat = w_one.shape[0]
    queries = wide // feat
    rel_count = rel_one.shape[0]
    n_d = lax.axis_size("dom")
    n_q = lax.axis_size("query")
    send = ghost_slots.shape[1]
    ghosts = n_d * send
    e_in, e_bd = edges_in.shape[1], edges_bd.shape[1]
    edges = e_in + e_bd
    rel_pad = -(-(rel_count + 1) // 128) * 128
    rel_rows = -(-(rel_count + 1) // 16) * 16
    width = -(-(rel_rows + feat) // 128) * 128
    grp = max(1, 8 // n_q)
    n_near, n_far = n_q * grp, n_d // grp
    part = feat // n_near
    scale_w = 1.0 / math.sqrt(rows * n_d * queries * n_q)
    scale_r = math.sqrt(rel_count / (n_d * edges * queries * n_q))

    args = (
        h_in,
        cotangent,
        w_one,
        w_two,
        rel_one.T,
        rel_two.T,
        query_emb.T,
        q_head,
        q_rel,
        bnd_rows[None, :],
        ghost_slots,
        edges_in,
        edges_bd,
    )
    spaces = [pltpu.VMEM] * 7 + [pltpu.SMEM] * 2 + [pltpu.VMEM] * 4

    vmem = pl.BlockSpec(memory_space=pltpu.VMEM)
    dma = pltpu.SemaphoreType.DMA
    shapes = (
        jax.ShapeDtypeStruct((rows, wide), F32),
        jax.ShapeDtypeStruct((2, feat, feat), F32),
        jax.ShapeDtypeStruct((2, feat, rel_count), F32),
    )
    results = pl.pallas_call(
        functools.partial(kernel, n_q, n_d, grp, scale_w, scale_r, rel_count, rel_rows),
        out_shape=tuple(pltpu.VMEM(s.shape, s.dtype) for s in shapes),
        in_specs=[pl.BlockSpec(memory_space=pltpu.HBM)] * len(args),
        out_specs=(vmem, vmem, vmem),
        scratch_shapes=[
            *(space(a.shape, a.dtype) for a, space in zip(args, spaces)),
            pltpu.VMEM((2 * feat, rel_pad), BF16),
            pltpu.VMEM((n_d, 1, 128), jnp.int32),
            pltpu.VMEM((rel_pad, edges), BF16),
            pltpu.VMEM((rows, edges), BF16),
            pltpu.VMEM((rows, e_in), BF16),
            pltpu.VMEM((ghosts, e_bd), BF16),
            pltpu.VMEM((2 * feat, edges), BF16),
            pltpu.VMEM((wide, edges), BF16),
            pltpu.VMEM((wide, edges), BF16),
            pltpu.VMEM((n_d, 1, 128), jnp.int32),
            pltpu.VMEM((ghosts, wide), BF16),
            pltpu.VMEM((ghosts, wide), BF16),
            pltpu.VMEM((ghosts, wide), BF16),
            pltpu.VMEM((ghosts, wide), BF16),
            pltpu.VMEM((ghosts, wide), BF16),
            pltpu.VMEM((ghosts, wide), BF16),
            pltpu.VMEM((ghosts, wide), BF16),
            pltpu.VMEM((ghosts, wide), BF16),
            pltpu.VMEM((2, n_near, part, width), BF16),
            pltpu.VMEM((2, n_near, part, width), BF16),
            pltpu.VMEM((2, n_far, part, width), BF16),
            pltpu.VMEM((2, n_near, part, width), BF16),
            dma((5,)),
            dma((5,)),
            dma((2, 3)),
            dma((2, 3)),
            dma((len(args),)),
        ],
        compiler_params=pltpu.CompilerParams(
            collective_id=0, has_side_effects=True, vmem_limit_bytes=33554432
        ),
    )(*(pltpu.with_memory_space_constraint(a, pltpu.HBM) for a in args))
    grad_in, grad_w, grad_rel_t = pl.pallas_call(
        write_out,
        out_shape=shapes,
        in_specs=[vmem] * 3,
        out_specs=[pl.BlockSpec(memory_space=pltpu.HBM)] * 3,
        scratch_shapes=[dma((3,))],
        compiler_params=pltpu.CompilerParams(vmem_limit_bytes=16777216),
    )(*results)
    return grad_in, grad_w, jnp.swapaxes(grad_rel_t, 1, 2)


def solution(mesh):
    return jax.shard_map(
        body,
        mesh=mesh,
        in_specs=(
            P("dom", "query"),
            P("dom", "query"),
            P(),
            P(),
            P(),
            P(),
            P(),
            P("query"),
            P("query"),
            P("dom"),
            P("dom", None),
            P(None, "dom"),
            P(None, "dom"),
        ),
        out_specs=(P("dom", "query"), P(), P()),
        check_vma=False,
    )
```

```python
import functools
import math

import jax
import jax.numpy as jnp
from jax import lax
from jax.experimental import pallas as pl
from jax.experimental.pallas import tpu as pltpu
from jax.sharding import PartitionSpec as P

MESH = pl.DeviceIdType.MESH
F32 = jnp.float32
BF16 = jnp.bfloat16
RS_EARLY = False


def dot_nn(a, b):
    return lax.dot_general(a, b, (((1,), (0,)), ((), ())), preferred_element_type=F32)


def dot_nt(a, b):
    return lax.dot_general(a, b, (((1,), (1,)), ((), ())), preferred_element_type=F32)


def split_hi_lo(x, axis):
    hi = x.astype(BF16)
    lo = (x - hi.astype(F32)).astype(BF16)
    return jnp.concatenate([hi, lo], axis=axis)


def onehot_into(dest, ids, col0, block):
    rows = dest.shape[0]
    count = ids.shape[1]

    def fill(i, carry):
        base = pl.multiple_of(i * block, block)
        row_ids = lax.broadcasted_iota(jnp.int32, (block, count), 0) + base
        dest[pl.ds(base, block), pl.ds(col0, count)] = jnp.where(row_ids == ids, 1.0, 0.0).astype(BF16)
        return carry

    lax.fori_loop(0, rows // block, fill, 0)


def loop(low, high, step):
    if high - low <= 32:
        for i in range(low, high):
            step(i, 0)
    else:
        lax.fori_loop(low, high, step, 0)


def div(a, b):
    return a // b if isinstance(a, int) else lax.div(a, b)


def rem(a, b):
    return a % b if isinstance(a, int) else lax.rem(a, b)


def aligned(a, b):
    return a if isinstance(a, int) else pl.multiple_of(a, b)


def kernel(
    n_q,
    n_d,
    grp,
    scale_w,
    scale_r,
    rel_count,
    rel_rows,
    *refs,
):
    n_in = 13
    hbm = refs[:n_in]
    gin_ref, gw_ref, grel_ref = refs[n_in : n_in + 3]
    local = refs[n_in + 3 : 2 * n_in + 3]
    (
        h_ref, cot_ref, w1_ref, w2_ref, r1_ref, r2_ref, qe_ref, qhead_ref, qrel_ref, bnd_ref, gs_ref, ein_ref, ebd_ref,
    ) = local
    (
    relt,
    gs_x,
    rt,
    vt,
    st_in,
    st_bd,
    rel_e,
    x1,
    x2,
    req,
    pub,
    pubs,
    pick_pub,
    out2,
    ghost2,
    ret_out2,
    ret_in2,
    ret_out1,
    ret_in1,
    red_src,
    red_in,
    red_z,
    red_all,
    xsend,
    xrecv,
    asend,
    arecv,
    load_sem,
    ) = refs[2 * n_in + 3 :]
    me_d = lax.axis_index("dom")
    me_q = lax.axis_index("query")
    n_far = n_d // grp
    n_near = n_q * grp
    far = lax.div(me_d, grp)
    near = lax.rem(me_d, grp)
    me_n = me_q * grp + near
    feat = w1_ref.shape[0]
    rows, wide = h_ref.shape
    queries = wide // feat
    send = ghost2.shape[0] // n_d
    slots = bnd_ref.shape[1]
    e_in = ein_ref.shape[1]
    e_bd = ebd_ref.shape[1]
    width = red_src.shape[3]

    barrier = pltpu.get_barrier_semaphore()

    def greet(i, carry):
        t = lax.rem(me_d + i, n_d)
        pl.semaphore_signal(barrier, inc=1, device_id=(me_q, t), device_id_type=MESH)
        return carry

    loop(1, n_d, greet)
    for dq in range(1, n_q):
        for k in range(grp):
            pl.semaphore_signal(
                barrier,
                inc=1,
                device_id=(lax.rem(me_q + dq, n_q), far * grp + k),
                device_id_type=MESH,
            )
    greeted = n_d - 1 + (n_q - 1) * grp
    loads = [
        pltpu.make_async_copy(src, dst, load_sem.at[k])
        for k, (src, dst) in enumerate(zip(hbm, local))
    ]
    for load in loads[::-1]:
        load.start()
    for load in loads[::-1]:
        load.wait()

    def peer_loop(step):
        if n_d <= 32:
            order = sorted(range(1, n_d), key=lambda i: -min(i // grp, n_far - i // grp))
            for i in order:
                step(i, 0)
        else:
            lax.fori_loop(1, n_d, step, 0)

    def exchange_start(phase, src, dst, size):
        def go(i, carry):
            peer = lax.rem(me_d + i, n_d)
            if size is None:
                s, d = src.at[peer], dst.at[me_d]
            else:
                s = src.at[pl.ds(pl.multiple_of(peer * size, size), size)]
                d = dst.at[pl.ds(pl.multiple_of(me_d * size, size), size)]
            pltpu.make_async_remote_copy(
                src_ref=s,
                dst_ref=d,
                send_sem=xsend.at[phase],
                recv_sem=xrecv.at[phase],
                device_id=(me_q, peer),
                device_id_type=MESH,
            ).start()
            return carry

        peer_loop(go)
        if size is None:
            dst[me_d] = src[me_d]
        else:
            own = pl.ds(pl.multiple_of(me_d * size, size), size)
            dst[own, :] = src[own, :]

    def spread_start(phase, src, dst, size):
        own = pl.ds(pl.multiple_of(me_d * size, size), size)

        def go(i, carry):
            pltpu.make_async_remote_copy(
                src_ref=src,
                dst_ref=dst.at[own],
                send_sem=xsend.at[phase],
                recv_sem=xrecv.at[phase],
                device_id=(me_q, lax.rem(me_d + i, n_d)),
                device_id_type=MESH,
            ).start()
            return carry

        peer_loop(go)
        dst[own, :] = src[...]

    def exchange_wait(phase, src, dst, size):
        some = pl.ds(0, (n_d - 1) * (size or 1))
        pltpu.make_async_remote_copy(
            src_ref=src.at[some],
            dst_ref=dst.at[some],
            send_sem=xsend.at[phase],
            recv_sem=xrecv.at[phase],
            device_id=(me_q, lax.rem(me_d + 1, n_d)),
            device_id_type=MESH,
        ).wait()

    def near_device(t):
        return lax.div(t, grp), far * grp + lax.rem(t, grp)

    def all_copy(layer, stage, src, dst, device):
        return pltpu.make_async_remote_copy(
            src_ref=src,
            dst_ref=dst,
            send_sem=asend.at[layer, stage],
            recv_sem=arecv.at[layer, stage],
            device_id=device,
            device_id_type=MESH,
        )

    def scatter_start(layer):
        def go(j, carry):
            t = lax.rem(me_n + j, n_near)
            all_copy(layer, 0, red_src.at[layer, t], red_in.at[layer, me_n], near_device(t)).start()
            return carry

        loop(1, n_near, go)

    def far_start(layer):
        some = pl.ds(0, n_near - 1)
        all_copy(
            layer, 0, red_src.at[layer, some], red_in.at[layer, some], near_device(lax.rem(me_n + 1, n_near))
        ).wait()
        red_in[layer, me_n] = red_src[layer, me_n]
        red_z[layer, far] = jnp.sum(red_in[layer].astype(F32), axis=0).astype(BF16)

        def go(j, carry):
            t = lax.rem(far + j, n_far)
            all_copy(layer, 1, red_z.at[layer, far], red_z.at[layer, far], (me_q, t * grp + near)).start()
            return carry

        loop(1, n_far, go)

    def gather_start(layer):
        if n_far > 1:
            some = pl.ds(0, n_far - 1)
            all_copy(
                layer,
                1,
                red_z.at[layer, some],
                red_z.at[layer, some],
                (me_q, lax.rem(far + 1, n_far) * grp + near),
            ).wait()
        red_all[layer, me_n] = jnp.sum(red_z[layer].astype(F32), axis=0).astype(BF16)

        def go(j, carry):
            t = lax.rem(me_n + j, n_near)
            all_copy(layer, 2, red_all.at[layer, me_n], red_all.at[layer, me_n], near_device(t)).start()
            return carry

        loop(1, n_near, go)

    def gather_wait(layer):
        some = pl.ds(0, n_near - 1)
        all_copy(
            layer, 2, red_all.at[layer, some], red_all.at[layer, some], near_device(lax.rem(me_n + 1, n_near))
        ).wait()

    def pack(layer, rg, wg):
        parts = [rg, wg]
        left = width - rel_rows - feat
        if left:
            parts.append(jnp.zeros((feat, left), F32))
        whole = jnp.concatenate(parts, axis=1)
        red_src[layer] = whole.reshape(n_near, feat // n_near, width).astype(BF16)

    def unpack(layer):
        summed = red_all[layer].astype(F32).reshape(feat, width)
        grel_ref[layer] = summed[:, :rel_count] * scale_r
        gw_ref[layer] = summed[:, rel_rows : rel_rows + feat] * scale_w

    per = 128 // send
    spread = jnp.concatenate([gs_ref[...]] * per, axis=1)
    for p in range(n_d):
        gs_x[p] = spread[p : p + 1, :]
    own_ids = lax.broadcasted_iota(jnp.int32, (rows, slots), 0)
    row_of32 = jnp.where(own_ids == bnd_ref[...], 1.0, 0.0)
    row_of = row_of32.astype(BF16)
    pub[...] = dot_nn(row_of32.T.astype(BF16), h_ref[...]).astype(BF16)

    onehot_into(vt, ein_ref[1:2, :], 0, 64)
    onehot_into(vt, ebd_ref[1:2, :], e_in, 64)
    pl.semaphore_wait(barrier, greeted)
    spread_start(1, pub, pubs, slots)
    exchange_start(0, gs_x, req, None)

    lane_group = lax.broadcasted_iota(jnp.int32, (1, 128), 1) // send

    def in_lanes(table):
        parts = []
        for j in range(n_d // per):
            vec = jnp.zeros((1, 128), jnp.int32)
            for k in range(per):
                vec = jnp.where(lane_group == k, table[j * per + k, 0:1, :], vec)
            parts.append(vec)
        return jnp.concatenate(parts, axis=1)

    ghost_peer = lax.broadcasted_iota(jnp.int32, (1, n_d * send), 1) // send
    pick_rows = in_lanes(gs_x) + ghost_peer * slots
    for j in range(n_d * send // 128):
        ids = pick_rows[:, j * 128 : (j + 1) * 128]
        for k in range(n_d * slots // 128):
            row_ids = lax.broadcasted_iota(jnp.int32, (128, 128), 0) + k * 128
            block = jnp.where(row_ids == ids, 1.0, 0.0).T
            pick_pub[pl.ds(j * 128, 128), pl.ds(k * 128, 128)] = block.astype(BF16)
    onehot_into(st_in, ein_ref[0:1, :], 0, 64)
    onehot_into(st_bd, ebd_ref[0:1, :], 0, 64)
    onehot_into(rt, ein_ref[2:3, :], 0, 32)
    onehot_into(rt, ebd_ref[2:3, :], e_in, 32)
    relt[...] = jnp.zeros_like(relt)
    relt[pl.ds(0, feat), pl.ds(0, rel_count)] = r1_ref[...]
    relt[pl.ds(feat, feat), pl.ds(0, rel_count)] = r2_ref[...]
    rel_e[...] = dot_nn(relt[...], rt[...]).astype(BF16)

    row_ids = lax.broadcasted_iota(jnp.int32, (feat, rows), 1) + me_d * rows
    lane_rel = lax.broadcasted_iota(jnp.int32, (feat, rel_count), 1)
    qtab = qe_ref[...].astype(F32)
    boost_parts = []
    for q in range(queries):
        vec = jnp.sum(jnp.where(lane_rel == qrel_ref[q], qtab, 0.0), axis=1, keepdims=True)
        boost_parts.append(jnp.where(row_ids == qhead_ref[q], vec, 0.0))
    boost = jnp.concatenate(boost_parts, axis=0)

    h32 = h_ref[...].astype(F32)
    h_t32 = h32.T
    h_t = h_t32.astype(BF16)

    def rel_tile(layer, lo, count):
        part = rel_e[pl.ds(layer * feat, feat), pl.ds(lo, count)].astype(F32)
        return jnp.concatenate([part] * queries, axis=0)

    def aggregate(layer, table_t, onehot, save, lo, count):
        sourced = dot_nn(table_t, onehot[...])
        save[:, pl.ds(lo, count)] = sourced.astype(BF16)
        message = split_hi_lo(sourced * rel_tile(layer, lo, count), 0)
        both = dot_nt(message, vt[:, pl.ds(lo, count)])
        return both[:wide] + both[wide:]

    def normalise(summed, w_ref):
        summed_b = summed.astype(BF16)
        normed, rstds = [], []
        for q in range(queries):
            mixed = lax.dot_general(
                w_ref[...],
                summed_b[q * feat : (q + 1) * feat],
                (((0,), (0,)), ((), ())),
                preferred_element_type=F32,
            )
            center = mixed - jnp.mean(mixed, axis=0, keepdims=True)
            rstd = lax.rsqrt(jnp.mean(center * center, axis=0, keepdims=True) + 1e-05)
            normed.append(center * rstd)
            rstds.append(rstd)
        return summed_b, normed, rstds

    def back_layer(up_t, normed, rstds, w_ref):
        dmixes, dsum = [], []
        for q in range(queries):
            y = normed[q]
            sig = jax.nn.sigmoid(y)
            dact = up_t[q * feat : (q + 1) * feat] * sig * (1.0 + y * (1.0 - sig))
            dmix = rstds[q] * (
                dact
                - jnp.mean(dact, axis=0, keepdims=True)
                - y * jnp.mean(dact * y, axis=0, keepdims=True)
            )
            dmix_b = dmix.astype(BF16)
            dmixes.append(dmix_b)
            dsum.append(dot_nn(w_ref[...], dmix_b).astype(BF16))
        return dmixes, jnp.concatenate(dsum, axis=0)

    def weight_grad(summed_b, dmixes):
        wgrad = jnp.zeros((feat, feat), F32)
        for q in range(queries):
            wgrad = wgrad + dot_nt(summed_b[q * feat : (q + 1) * feat], dmixes[q])
        return wgrad

    def rel_grad(downs, save):
        tots = []
        lo = 0
        for down in downs:
            count = down.shape[1]
            prod = down * save[:, pl.ds(lo, count)].astype(F32)
            tot = prod[:feat]
            for q in range(1, queries):
                tot = tot + prod[q * feat : (q + 1) * feat]
            tots.append(split_hi_lo(tot, 0))
            lo += count
        both = dot_nt(jnp.concatenate(tots, axis=1), rt[pl.ds(0, rel_rows), :])
        return both[:feat] + both[feat:]

    def table_grad(layer, down, onehot, lo, count):
        message = (down * rel_tile(layer, lo, count)).astype(BF16)
        return dot_nt(onehot[...], message)

    def give_back(ret_in):
        return dot_nn(pick_t, ret_in[...])

    sum1 = aggregate(0, h_t, st_in, x1, 0, e_in) + boost
    exchange_wait(0, gs_x, req, None)
    slot_ids = lax.broadcasted_iota(jnp.int32, (slots, n_d * send), 0)
    slot_of32 = jnp.where(slot_ids == in_lanes(req), 1.0, 0.0)
    pick_t = dot_nn(row_of, slot_of32.astype(BF16)).astype(BF16)
    pick = dot_nt(slot_of32.T.astype(BF16), row_of).astype(BF16)
    exchange_wait(1, pubs, pubs, slots)
    ghost1_t = dot_nn(pick_pub[...], pubs[...]).T.astype(BF16)
    sum1 = sum1 + aggregate(0, ghost1_t, st_bd, x1, e_in, e_bd)
    sum1_b, norm1, rstd1 = normalise(sum1, w1_ref)
    h2_t = (
        jnp.concatenate([y * jax.nn.sigmoid(y) for y in norm1], axis=0) + h_t32
    ).astype(BF16)

    out2[...] = dot_nt(pick, h2_t).astype(BF16)
    exchange_start(2, out2, ghost2, send)
    sum2 = aggregate(1, h2_t, st_in, x2, 0, e_in) + boost
    exchange_wait(2, out2, ghost2, send)
    sum2 = sum2 + aggregate(1, ghost2[...].astype(F32).T.astype(BF16), st_bd, x2, e_in, e_bd)
    sum2_b, norm2, rstd2 = normalise(sum2, w2_ref)

    cot32 = cot_ref[...].astype(F32)
    dmix2, dsum2 = back_layer(cot32.T, norm2, rstd2, w2_ref)
    down2_bd = dot_nn(dsum2, vt[:, pl.ds(e_in, e_bd)])
    ret_out2[...] = table_grad(1, down2_bd, st_bd, e_in, e_bd).astype(BF16)
    exchange_start(3, ret_out2, ret_in2, send)
    down2_in = dot_nn(dsum2, vt[:, pl.ds(0, e_in)])
    mid = cot32 + table_grad(1, down2_in, st_in, 0, e_in)
    pack(1, rel_grad((down2_in, down2_bd), x2), weight_grad(sum2_b, dmix2))
    if RS_EARLY:
        scatter_start(1)
    exchange_wait(3, ret_out2, ret_in2, send)
    if not RS_EARLY:
        scatter_start(1)
    mid = mid + give_back(ret_in2)

    dmix1, dsum1 = back_layer(mid.T, norm1, rstd1, w1_ref)
    down1_in = dot_nn(dsum1, vt[:, pl.ds(0, e_in)])
    down1_bd = dot_nn(dsum1, vt[:, pl.ds(e_in, e_bd)])
    pack(0, rel_grad((down1_in, down1_bd), x1), weight_grad(sum1_b, dmix1))
    scatter_start(0)
    far_start(1)
    ret_out1[...] = table_grad(0, down1_bd, st_bd, e_in, e_bd).astype(BF16)
    exchange_start(4, ret_out1, ret_in1, send)
    base = mid + table_grad(0, down1_in, st_in, 0, e_in)
    far_start(0)
    gather_start(1)
    exchange_wait(4, ret_out1, ret_in1, send)
    gin_ref[...] = base + give_back(ret_in1)
    gather_start(0)
    gather_wait(1)
    unpack(1)
    gather_wait(0)
    unpack(0)


def write_out(*refs):
    half = (len(refs) - 1) // 2
    copies = [
        pltpu.make_async_copy(src, dst, refs[-1].at[k])
        for k, (src, dst) in enumerate(zip(refs[:half], refs[half : 2 * half]))
    ]
    for copy in copies:
        copy.start()
    for copy in copies:
        copy.wait()


def body(
    h_in,
    cotangent,
    w_one,
    w_two,
    rel_one,
    rel_two,
    query_emb,
    q_head,
    q_rel,
    bnd_rows,
    ghost_slots,
    edges_in,
    edges_bd,
):
    rows, wide = h_in.shape
    feat = w_one.shape[0]
    queries = wide // feat
    rel_count = rel_one.shape[0]
    n_d = lax.axis_size("dom")
    n_q = lax.axis_size("query")
    send = ghost_slots.shape[1]
    ghosts = n_d * send
    slots = bnd_rows.shape[0]
    e_in, e_bd = edges_in.shape[1], edges_bd.shape[1]
    edges = e_in + e_bd
    rel_pad = -(-(rel_count + 1) // 128) * 128
    rel_rows = -(-(rel_count + 1) // 16) * 16
    width = -(-(rel_rows + feat) // 128) * 128
    grp = max(1, 8 // n_q)
    n_near, n_far = n_q * grp, n_d // grp
    part = feat // n_near
    scale_w = 1.0 / math.sqrt(rows * n_d * queries * n_q)
    scale_r = math.sqrt(rel_count / (n_d * edges * queries * n_q))

    args = (
        h_in,
        cotangent,
        w_one,
        w_two,
        rel_one.T,
        rel_two.T,
        query_emb.T,
        q_head,
        q_rel,
        bnd_rows[None, :],
        ghost_slots,
        edges_in,
        edges_bd,
    )
    spaces = [pltpu.VMEM] * 7 + [pltpu.SMEM] * 2 + [pltpu.VMEM] * 4

    vmem = pl.BlockSpec(memory_space=pltpu.VMEM)
    dma = pltpu.SemaphoreType.DMA
    shapes = (
        jax.ShapeDtypeStruct((rows, wide), F32),
        jax.ShapeDtypeStruct((2, feat, feat), F32),
        jax.ShapeDtypeStruct((2, feat, rel_count), F32),
    )
    results = pl.pallas_call(
        functools.partial(kernel, n_q, n_d, grp, scale_w, scale_r, rel_count, rel_rows),
        out_shape=tuple(pltpu.VMEM(s.shape, s.dtype) for s in shapes),
        in_specs=[pl.BlockSpec(memory_space=pltpu.HBM)] * len(args),
        out_specs=(vmem, vmem, vmem),
        scratch_shapes=[
            *(space(a.shape, a.dtype) for a, space in zip(args, spaces)),
            pltpu.VMEM((2 * feat, rel_pad), BF16),
            pltpu.VMEM((n_d, 1, 128), jnp.int32),
            pltpu.VMEM((rel_pad, edges), BF16),
            pltpu.VMEM((rows, edges), BF16),
            pltpu.VMEM((rows, e_in), BF16),
            pltpu.VMEM((ghosts, e_bd), BF16),
            pltpu.VMEM((2 * feat, edges), BF16),
            pltpu.VMEM((wide, edges), BF16),
            pltpu.VMEM((wide, edges), BF16),
            pltpu.VMEM((n_d, 1, 128), jnp.int32),
            pltpu.VMEM((slots, wide), BF16),
            pltpu.VMEM((n_d * slots, wide), BF16),
            pltpu.VMEM((ghosts, n_d * slots), BF16),
            pltpu.VMEM((ghosts, wide), BF16),
            pltpu.VMEM((ghosts, wide), BF16),
            pltpu.VMEM((ghosts, wide), BF16),
            pltpu.VMEM((ghosts, wide), BF16),
            pltpu.VMEM((ghosts, wide), BF16),
            pltpu.VMEM((ghosts, wide), BF16),
            pltpu.VMEM((2, n_near, part, width), BF16),
            pltpu.VMEM((2, n_near, part, width), BF16),
            pltpu.VMEM((2, n_far, part, width), BF16),
            pltpu.VMEM((2, n_near, part, width), BF16),
            dma((5,)),
            dma((5,)),
            dma((2, 3)),
            dma((2, 3)),
            dma((len(args),)),
        ],
        compiler_params=pltpu.CompilerParams(
            collective_id=0, has_side_effects=True, vmem_limit_bytes=33554432
        ),
    )(*(pltpu.with_memory_space_constraint(a, pltpu.HBM) for a in args))
    grad_in, grad_w, grad_rel_t = pl.pallas_call(
        write_out,
        out_shape=shapes,
        in_specs=[vmem] * 3,
        out_specs=[pl.BlockSpec(memory_space=pltpu.HBM)] * 3,
        scratch_shapes=[dma((3,))],
        compiler_params=pltpu.CompilerParams(vmem_limit_bytes=16777216),
    )(*results)
    return grad_in, grad_w, jnp.swapaxes(grad_rel_t, 1, 2)


def solution(mesh):
    return jax.shard_map(
        body,
        mesh=mesh,
        in_specs=(
            P("dom", "query"),
            P("dom", "query"),
            P(),
            P(),
            P(),
            P(),
            P(),
            P("query"),
            P("query"),
            P("dom"),
            P("dom", None),
            P(None, "dom"),
            P(None, "dom"),
        ),
        out_specs=(P("dom", "query"), P(), P()),
        check_vma=False,
    )
```

```python
import functools
import math

import jax
import jax.numpy as jnp
from jax import lax
from jax.experimental import pallas as pl
from jax.experimental.pallas import tpu as pltpu
from jax.sharding import PartitionSpec as P

MESH = pl.DeviceIdType.MESH
F32 = jnp.float32
BF16 = jnp.bfloat16


def dot_nn(a, b):
    return lax.dot_general(a, b, (((1,), (0,)), ((), ())), preferred_element_type=F32)


def dot_nt(a, b):
    return lax.dot_general(a, b, (((1,), (1,)), ((), ())), preferred_element_type=F32)


def split_hi_lo(x, axis):
    hi = x.astype(BF16)
    lo = (x - hi.astype(F32)).astype(BF16)
    return jnp.concatenate([hi, lo], axis=axis)


def onehot_into(dest, ids, col0, block):
    rows = dest.shape[0]
    count = ids.shape[1]

    def fill(i, carry):
        base = pl.multiple_of(i * block, block)
        row_ids = lax.broadcasted_iota(jnp.int32, (block, count), 0) + base
        dest[pl.ds(base, block), pl.ds(col0, count)] = jnp.where(row_ids == ids, 1.0, 0.0).astype(BF16)
        return carry

    lax.fori_loop(0, rows // block, fill, 0)


def loop(low, high, step):
    if high - low <= 32:
        for i in range(low, high):
            step(i, 0)
    else:
        lax.fori_loop(low, high, step, 0)


def div(a, b):
    return a // b if isinstance(a, int) else lax.div(a, b)


def rem(a, b):
    return a % b if isinstance(a, int) else lax.rem(a, b)


def aligned(a, b):
    return a if isinstance(a, int) else pl.multiple_of(a, b)


def kernel(
    n_q,
    n_d,
    grp,
    scale_w,
    scale_r,
    rel_count,
    rel_rows,
    *refs,
):
    n_in = 13
    hbm = refs[:n_in]
    gin_ref, gw_ref, grel_ref = refs[n_in : n_in + 3]
    local = refs[n_in + 3 : 2 * n_in + 3]
    (
        h_ref, cot_ref, w1_ref, w2_ref, r1_ref, r2_ref, qe_ref, qhead_ref, qrel_ref, bnd_ref, gs_ref, ein_ref, ebd_ref,
    ) = local
    (
    relt,
    gs_x,
    rt,
    vt,
    st_in,
    st_bd,
    rel_e,
    x1,
    x2,
    req,
    out1,
    ghost1,
    out2,
    ghost2,
    ret_out2,
    ret_in2,
    ret_out1,
    ret_in1,
    red_src,
    red_in,
    red_z,
    red_all,
    xsend,
    xrecv,
    asend,
    arecv,
    load_sem,
    ) = refs[2 * n_in + 3 :]
    me_d = lax.axis_index("dom")
    me_q = lax.axis_index("query")
    n_far = n_d // grp
    n_near = n_q * grp
    far = lax.div(me_d, grp)
    near = lax.rem(me_d, grp)
    me_n = me_q * grp + near
    feat = w1_ref.shape[0]
    rows, wide = h_ref.shape
    queries = wide // feat
    send = ghost1.shape[0] // n_d
    e_in = ein_ref.shape[1]
    e_bd = ebd_ref.shape[1]
    width = red_src.shape[3]

    def peer_loop(step):
        if n_d <= 32:
            order = sorted(range(1, n_d), key=lambda i: -min(i // grp, n_far - i // grp))
            for i in order:
                step(i, 0)
        else:
            lax.fori_loop(1, n_d, step, 0)

    barrier = pltpu.get_barrier_semaphore()

    def greet(i, carry):
        t = lax.rem(me_d + i, n_d)
        pl.semaphore_signal(barrier, inc=1, device_id=(me_q, t), device_id_type=MESH)
        return carry

    peer_loop(greet)
    for dq in range(1, n_q):
        for k in range(grp):
            pl.semaphore_signal(
                barrier,
                inc=1,
                device_id=(lax.rem(me_q + dq, n_q), far * grp + k),
                device_id_type=MESH,
            )
    greeted = n_d - 1 + (n_q - 1) * grp
    loads = [
        pltpu.make_async_copy(src, dst, load_sem.at[k])
        for k, (src, dst) in enumerate(zip(hbm, local))
    ]
    for load in loads[::-1]:
        load.start()
    for load in loads[::-1]:
        load.wait()

    def exchange_start(phase, src, dst, size):
        def go(i, carry):
            peer = lax.rem(me_d + i, n_d)
            if size is None:
                s, d = src.at[peer], dst.at[me_d]
            else:
                s = src.at[pl.ds(pl.multiple_of(peer * size, size), size)]
                d = dst.at[pl.ds(pl.multiple_of(me_d * size, size), size)]
            pltpu.make_async_remote_copy(
                src_ref=s,
                dst_ref=d,
                send_sem=xsend.at[phase],
                recv_sem=xrecv.at[phase],
                device_id=(me_q, peer),
                device_id_type=MESH,
            ).start()
            return carry

        peer_loop(go)
        if size is None:
            dst[me_d] = src[me_d]
        else:
            own = pl.ds(pl.multiple_of(me_d * size, size), size)
            dst[own, :] = src[own, :]

    def exchange_wait(phase, src, dst, size):
        some = pl.ds(0, (n_d - 1) * (size or 1))
        pltpu.make_async_remote_copy(
            src_ref=src.at[some],
            dst_ref=dst.at[some],
            send_sem=xsend.at[phase],
            recv_sem=xrecv.at[phase],
            device_id=(me_q, lax.rem(me_d + 1, n_d)),
            device_id_type=MESH,
        ).wait()

    def near_device(t):
        return lax.div(t, grp), far * grp + lax.rem(t, grp)

    def all_copy(layer, stage, src, dst, device):
        return pltpu.make_async_remote_copy(
            src_ref=src,
            dst_ref=dst,
            send_sem=asend.at[layer, stage],
            recv_sem=arecv.at[layer, stage],
            device_id=device,
            device_id_type=MESH,
        )

    def scatter_start(layer):
        def go(j, carry):
            t = lax.rem(me_n + j, n_near)
            all_copy(layer, 0, red_src.at[layer, t], red_in.at[layer, me_n], near_device(t)).start()
            return carry

        loop(1, n_near, go)

    def far_start(layer):
        some = pl.ds(0, n_near - 1)
        all_copy(
            layer, 0, red_src.at[layer, some], red_in.at[layer, some], near_device(lax.rem(me_n + 1, n_near))
        ).wait()
        red_in[layer, me_n] = red_src[layer, me_n]
        red_z[layer, far] = jnp.sum(red_in[layer].astype(F32), axis=0).astype(BF16)

        def go(j, carry):
            t = lax.rem(far + j, n_far)
            all_copy(layer, 1, red_z.at[layer, far], red_z.at[layer, far], (me_q, t * grp + near)).start()
            return carry

        loop(1, n_far, go)

    def gather_start(layer):
        if n_far > 1:
            some = pl.ds(0, n_far - 1)
            all_copy(
                layer,
                1,
                red_z.at[layer, some],
                red_z.at[layer, some],
                (me_q, lax.rem(far + 1, n_far) * grp + near),
            ).wait()
        red_all[layer, me_n] = jnp.sum(red_z[layer].astype(F32), axis=0).astype(BF16)

        def go(j, carry):
            t = lax.rem(me_n + j, n_near)
            all_copy(layer, 2, red_all.at[layer, me_n], red_all.at[layer, me_n], near_device(t)).start()
            return carry

        loop(1, n_near, go)

    def gather_wait(layer):
        some = pl.ds(0, n_near - 1)
        all_copy(
            layer, 2, red_all.at[layer, some], red_all.at[layer, some], near_device(lax.rem(me_n + 1, n_near))
        ).wait()

    def pack(layer, rg, wg):
        parts = [rg, wg]
        left = width - rel_rows - feat
        if left:
            parts.append(jnp.zeros((feat, left), F32))
        whole = jnp.concatenate(parts, axis=1)
        red_src[layer] = whole.reshape(n_near, feat // n_near, width).astype(BF16)

    def unpack(layer):
        summed = red_all[layer].astype(F32).reshape(feat, width)
        grel_ref[layer] = summed[:, :rel_count] * scale_r
        gw_ref[layer] = summed[:, rel_rows : rel_rows + feat] * scale_w

    per = 128 // send
    spread = jnp.concatenate([gs_ref[...]] * per, axis=1)
    for p in range(n_d):
        gs_x[p] = spread[p : p + 1, :]

    onehot_into(vt, ein_ref[1:2, :], 0, 64)
    onehot_into(vt, ebd_ref[1:2, :], e_in, 64)
    pl.semaphore_wait(barrier, greeted)
    exchange_start(0, gs_x, req, None)
    onehot_into(st_in, ein_ref[0:1, :], 0, 64)
    onehot_into(st_bd, ebd_ref[0:1, :], 0, 64)

    slots = bnd_ref.shape[1]
    own_ids = lax.broadcasted_iota(jnp.int32, (rows, slots), 0)
    row_of32 = jnp.where(own_ids == bnd_ref[...], 1.0, 0.0)
    row_of = row_of32.astype(BF16)
    published = dot_nn(row_of32.T.astype(BF16), h_ref[...]).astype(BF16)

    exchange_wait(0, gs_x, req, None)
    lane_group = lax.broadcasted_iota(jnp.int32, (1, 128), 1) // send
    wanted = []
    for j in range(n_d // per):
        vec = jnp.zeros((1, 128), jnp.int32)
        for k in range(per):
            vec = jnp.where(lane_group == k, req[j * per + k, 0:1, :], vec)
        wanted.append(vec)
    wanted = jnp.concatenate(wanted, axis=1)
    slot_ids = lax.broadcasted_iota(jnp.int32, (slots, n_d * send), 0)
    slot_of32 = jnp.where(slot_ids == wanted, 1.0, 0.0)
    slot_of_t = slot_of32.T.astype(BF16)
    out1[...] = dot_nn(slot_of_t, published).astype(BF16)
    exchange_start(1, out1, ghost1, send)

    onehot_into(rt, ein_ref[2:3, :], 0, 32)
    onehot_into(rt, ebd_ref[2:3, :], e_in, 32)
    relt[...] = jnp.zeros_like(relt)
    relt[pl.ds(0, feat), pl.ds(0, rel_count)] = r1_ref[...]
    relt[pl.ds(feat, feat), pl.ds(0, rel_count)] = r2_ref[...]
    rel_e[...] = dot_nn(relt[...], rt[...]).astype(BF16)
    pick_t = dot_nn(row_of, slot_of32.astype(BF16)).astype(BF16)
    pick = dot_nt(slot_of_t, row_of).astype(BF16)

    row_ids = lax.broadcasted_iota(jnp.int32, (feat, rows), 1) + me_d * rows
    lane_rel = lax.broadcasted_iota(jnp.int32, (feat, rel_count), 1)
    qtab = qe_ref[...].astype(F32)
    boost_parts = []
    for q in range(queries):
        vec = jnp.sum(jnp.where(lane_rel == qrel_ref[q], qtab, 0.0), axis=1, keepdims=True)
        boost_parts.append(jnp.where(row_ids == qhead_ref[q], vec, 0.0))
    boost = jnp.concatenate(boost_parts, axis=0)

    h32 = h_ref[...].astype(F32)
    h_t32 = h32.T
    h_t = h_t32.astype(BF16)

    def rel_tile(layer, lo, count):
        part = rel_e[pl.ds(layer * feat, feat), pl.ds(lo, count)].astype(F32)
        return jnp.concatenate([part] * queries, axis=0)

    def aggregate(layer, table_t, onehot, save, lo, count):
        sourced = dot_nn(table_t, onehot[...])
        save[:, pl.ds(lo, count)] = sourced.astype(BF16)
        message = split_hi_lo(sourced * rel_tile(layer, lo, count), 0)
        both = dot_nt(message, vt[:, pl.ds(lo, count)])
        return both[:wide] + both[wide:]

    def normalise(summed, w_ref):
        summed_b = summed.astype(BF16)
        normed, rstds = [], []
        for q in range(queries):
            mixed = lax.dot_general(
                w_ref[...],
                summed_b[q * feat : (q + 1) * feat],
                (((0,), (0,)), ((), ())),
                preferred_element_type=F32,
            )
            center = mixed - jnp.mean(mixed, axis=0, keepdims=True)
            rstd = lax.rsqrt(jnp.mean(center * center, axis=0, keepdims=True) + 1e-05)
            normed.append(center * rstd)
            rstds.append(rstd)
        return summed_b, normed, rstds

    def back_layer(up_t, normed, rstds, w_ref):
        dmixes, dsum = [], []
        for q in range(queries):
            y = normed[q]
            sig = jax.nn.sigmoid(y)
            dact = up_t[q * feat : (q + 1) * feat] * sig * (1.0 + y * (1.0 - sig))
            dmix = rstds[q] * (
                dact
                - jnp.mean(dact, axis=0, keepdims=True)
                - y * jnp.mean(dact * y, axis=0, keepdims=True)
            )
            dmix_b = dmix.astype(BF16)
            dmixes.append(dmix_b)
            dsum.append(dot_nn(w_ref[...], dmix_b).astype(BF16))
        return dmixes, jnp.concatenate(dsum, axis=0)

    def weight_grad(summed_b, dmixes):
        wgrad = jnp.zeros((feat, feat), F32)
        for q in range(queries):
            wgrad = wgrad + dot_nt(summed_b[q * feat : (q + 1) * feat], dmixes[q])
        return wgrad

    def rel_grad(downs, save):
        tots = []
        lo = 0
        for down in downs:
            count = down.shape[1]
            prod = down * save[:, pl.ds(lo, count)].astype(F32)
            tot = prod[:feat]
            for q in range(1, queries):
                tot = tot + prod[q * feat : (q + 1) * feat]
            tots.append(split_hi_lo(tot, 0))
            lo += count
        both = dot_nt(jnp.concatenate(tots, axis=1), rt[pl.ds(0, rel_rows), :])
        return both[:feat] + both[feat:]

    def table_grad(layer, down, onehot, lo, count):
        message = (down * rel_tile(layer, lo, count)).astype(BF16)
        return dot_nt(onehot[...], message)

    def give_back(ret_in):
        return dot_nn(pick_t, ret_in[...])

    sum1 = aggregate(0, h_t, st_in, x1, 0, e_in) + boost
    exchange_wait(1, out1, ghost1, send)
    sum1 = sum1 + aggregate(0, ghost1[...].astype(F32).T.astype(BF16), st_bd, x1, e_in, e_bd)
    sum1_b, norm1, rstd1 = normalise(sum1, w1_ref)
    h2_t = (
        jnp.concatenate([y * jax.nn.sigmoid(y) for y in norm1], axis=0) + h_t32
    ).astype(BF16)

    out2[...] = dot_nt(pick, h2_t).astype(BF16)
    exchange_start(2, out2, ghost2, send)
    sum2 = aggregate(1, h2_t, st_in, x2, 0, e_in) + boost
    exchange_wait(2, out2, ghost2, send)
    sum2 = sum2 + aggregate(1, ghost2[...].astype(F32).T.astype(BF16), st_bd, x2, e_in, e_bd)
    sum2_b, norm2, rstd2 = normalise(sum2, w2_ref)

    cot32 = cot_ref[...].astype(F32)
    dmix2, dsum2 = back_layer(cot32.T, norm2, rstd2, w2_ref)
    down2_bd = dot_nn(dsum2, vt[:, pl.ds(e_in, e_bd)])
    ret_out2[...] = table_grad(1, down2_bd, st_bd, e_in, e_bd).astype(BF16)
    exchange_start(3, ret_out2, ret_in2, send)
    down2_in = dot_nn(dsum2, vt[:, pl.ds(0, e_in)])
    pack(1, rel_grad((down2_in, down2_bd), x2), weight_grad(sum2_b, dmix2))
    scatter_start(1)
    mid = cot32 + table_grad(1, down2_in, st_in, 0, e_in)
    exchange_wait(3, ret_out2, ret_in2, send)
    mid = mid + give_back(ret_in2)

    dmix1, dsum1 = back_layer(mid.T, norm1, rstd1, w1_ref)
    down1_in = dot_nn(dsum1, vt[:, pl.ds(0, e_in)])
    down1_bd = dot_nn(dsum1, vt[:, pl.ds(e_in, e_bd)])
    pack(0, rel_grad((down1_in, down1_bd), x1), weight_grad(sum1_b, dmix1))
    scatter_start(0)
    far_start(1)
    ret_out1[...] = table_grad(0, down1_bd, st_bd, e_in, e_bd).astype(BF16)
    exchange_start(4, ret_out1, ret_in1, send)
    base = mid + table_grad(0, down1_in, st_in, 0, e_in)
    far_start(0)
    gather_start(1)
    exchange_wait(4, ret_out1, ret_in1, send)
    gin_ref[...] = base + give_back(ret_in1)
    gather_start(0)
    gather_wait(1)
    unpack(1)
    gather_wait(0)
    unpack(0)


def write_out(*refs):
    half = (len(refs) - 1) // 2
    copies = [
        pltpu.make_async_copy(src, dst, refs[-1].at[k])
        for k, (src, dst) in enumerate(zip(refs[:half], refs[half : 2 * half]))
    ]
    for copy in copies:
        copy.start()
    for copy in copies:
        copy.wait()


def body(
    h_in,
    cotangent,
    w_one,
    w_two,
    rel_one,
    rel_two,
    query_emb,
    q_head,
    q_rel,
    bnd_rows,
    ghost_slots,
    edges_in,
    edges_bd,
):
    rows, wide = h_in.shape
    feat = w_one.shape[0]
    queries = wide // feat
    rel_count = rel_one.shape[0]
    n_d = lax.axis_size("dom")
    n_q = lax.axis_size("query")
    send = ghost_slots.shape[1]
    ghosts = n_d * send
    e_in, e_bd = edges_in.shape[1], edges_bd.shape[1]
    edges = e_in + e_bd
    rel_pad = -(-(rel_count + 1) // 128) * 128
    rel_rows = -(-(rel_count + 1) // 16) * 16
    width = -(-(rel_rows + feat) // 128) * 128
    grp = max(1, 8 // n_q)
    n_near, n_far = n_q * grp, n_d // grp
    part = feat // n_near
    scale_w = 1.0 / math.sqrt(rows * n_d * queries * n_q)
    scale_r = math.sqrt(rel_count / (n_d * edges * queries * n_q))

    args = (
        h_in,
        cotangent,
        w_one,
        w_two,
        rel_one.T,
        rel_two.T,
        query_emb.T,
        q_head,
        q_rel,
        bnd_rows[None, :],
        ghost_slots,
        edges_in,
        edges_bd,
    )
    spaces = [pltpu.VMEM] * 7 + [pltpu.SMEM] * 2 + [pltpu.VMEM] * 4

    vmem = pl.BlockSpec(memory_space=pltpu.VMEM)
    dma = pltpu.SemaphoreType.DMA
    shapes = (
        jax.ShapeDtypeStruct((rows, wide), F32),
        jax.ShapeDtypeStruct((2, feat, feat), F32),
        jax.ShapeDtypeStruct((2, feat, rel_count), F32),
    )
    results = pl.pallas_call(
        functools.partial(kernel, n_q, n_d, grp, scale_w, scale_r, rel_count, rel_rows),
        out_shape=tuple(pltpu.VMEM(s.shape, s.dtype) for s in shapes),
        in_specs=[pl.BlockSpec(memory_space=pltpu.HBM)] * len(args),
        out_specs=(vmem, vmem, vmem),
        scratch_shapes=[
            *(space(a.shape, a.dtype) for a, space in zip(args, spaces)),
            pltpu.VMEM((2 * feat, rel_pad), BF16),
            pltpu.VMEM((n_d, 1, 128), jnp.int32),
            pltpu.VMEM((rel_pad, edges), BF16),
            pltpu.VMEM((rows, edges), BF16),
            pltpu.VMEM((rows, e_in), BF16),
            pltpu.VMEM((ghosts, e_bd), BF16),
            pltpu.VMEM((2 * feat, edges), BF16),
            pltpu.VMEM((wide, edges), BF16),
            pltpu.VMEM((wide, edges), BF16),
            pltpu.VMEM((n_d, 1, 128), jnp.int32),
            pltpu.VMEM((ghosts, wide), BF16),
            pltpu.VMEM((ghosts, wide), BF16),
            pltpu.VMEM((ghosts, wide), BF16),
            pltpu.VMEM((ghosts, wide), BF16),
            pltpu.VMEM((ghosts, wide), BF16),
            pltpu.VMEM((ghosts, wide), BF16),
            pltpu.VMEM((ghosts, wide), BF16),
            pltpu.VMEM((ghosts, wide), BF16),
            pltpu.VMEM((2, n_near, part, width), BF16),
            pltpu.VMEM((2, n_near, part, width), BF16),
            pltpu.VMEM((2, n_far, part, width), BF16),
            pltpu.VMEM((2, n_near, part, width), BF16),
            dma((5,)),
            dma((5,)),
            dma((2, 3)),
            dma((2, 3)),
            dma((len(args),)),
        ],
        compiler_params=pltpu.CompilerParams(
            collective_id=0, has_side_effects=True, vmem_limit_bytes=33554432
        ),
    )(*(pltpu.with_memory_space_constraint(a, pltpu.HBM) for a in args))
    grad_in, grad_w, grad_rel_t = pl.pallas_call(
        write_out,
        out_shape=shapes,
        in_specs=[vmem] * 3,
        out_specs=[pl.BlockSpec(memory_space=pltpu.HBM)] * 3,
        scratch_shapes=[dma((3,))],
        compiler_params=pltpu.CompilerParams(vmem_limit_bytes=16777216),
    )(*results)
    return grad_in, grad_w, jnp.swapaxes(grad_rel_t, 1, 2)


def solution(mesh):
    return jax.shard_map(
        body,
        mesh=mesh,
        in_specs=(
            P("dom", "query"),
            P("dom", "query"),
            P(),
            P(),
            P(),
            P(),
            P(),
            P("query"),
            P("query"),
            P("dom"),
            P("dom", None),
            P(None, "dom"),
            P(None, "dom"),
        ),
        out_specs=(P("dom", "query"), P(), P()),
        check_vma=False,
    )
```

```python
import functools
import math

import jax
import jax.numpy as jnp
from jax import lax
from jax.experimental import pallas as pl
from jax.experimental.pallas import tpu as pltpu
from jax.sharding import PartitionSpec as P

MESH = pl.DeviceIdType.MESH
F32 = jnp.float32
BF16 = jnp.bfloat16


def dot_nn(a, b):
    return lax.dot_general(a, b, (((1,), (0,)), ((), ())), preferred_element_type=F32)


def dot_nt(a, b):
    return lax.dot_general(a, b, (((1,), (1,)), ((), ())), preferred_element_type=F32)


def split_hi_lo(x, axis):
    hi = x.astype(BF16)
    lo = (x - hi.astype(F32)).astype(BF16)
    return jnp.concatenate([hi, lo], axis=axis)


def onehot_into(dest, ids, col0, block):
    rows = dest.shape[0]
    count = ids.shape[1]

    def fill(i, carry):
        base = pl.multiple_of(i * block, block)
        row_ids = lax.broadcasted_iota(jnp.int32, (block, count), 0) + base
        dest[pl.ds(base, block), pl.ds(col0, count)] = jnp.where(row_ids == ids, 1.0, 0.0).astype(BF16)
        return carry

    lax.fori_loop(0, rows // block, fill, 0)


def loop(low, high, step):
    if high - low <= 32:
        for i in range(low, high):
            step(i, 0)
    else:
        lax.fori_loop(low, high, step, 0)


def div(a, b):
    return a // b if isinstance(a, int) else lax.div(a, b)


def rem(a, b):
    return a % b if isinstance(a, int) else lax.rem(a, b)


def aligned(a, b):
    return a if isinstance(a, int) else pl.multiple_of(a, b)


def kernel(
    n_q,
    n_d,
    grp,
    scale_w,
    scale_r,
    rel_count,
    rel_rows,
    *refs,
):
    n_in = 13
    hbm = refs[:n_in]
    gin_ref, gw_ref, grel_ref = refs[n_in : n_in + 3]
    local = refs[n_in + 3 : 2 * n_in + 3]
    (
        h_ref, cot_ref, w1_ref, w2_ref, r1_ref, r2_ref, qe_ref, qhead_ref, qrel_ref, bnd_ref, gs_ref, ein_ref, ebd_ref,
    ) = local
    (
    relt,
    gs_x,
    rt,
    vt,
    st_in,
    st_bd,
    rel_e,
    x1,
    x2,
    req,
    out1,
    ghost1,
    out2,
    ghost2,
    ret_out2,
    ret_in2,
    ret_out1,
    ret_in1,
    red_src,
    red_in,
    red_z,
    red_all,
    xsend,
    xrecv,
    asend,
    arecv,
    load_sem,
    ) = refs[2 * n_in + 3 :]
    me_d = lax.axis_index("dom")
    me_q = lax.axis_index("query")
    n_far = n_d // grp
    n_near = n_q * grp
    far = lax.div(me_d, grp)
    near = lax.rem(me_d, grp)
    me_n = me_q * grp + near
    feat = w1_ref.shape[0]
    rows, wide = h_ref.shape
    queries = wide // feat
    send = ghost1.shape[0] // n_d
    e_in = ein_ref.shape[1]
    e_bd = ebd_ref.shape[1]
    width = red_src.shape[3]

    def peer_loop(step):
        if n_d <= 32:
            order = sorted(range(1, n_d), key=lambda i: -min(i // grp, n_far - i // grp))
            for i in order:
                step(i, 0)
        else:
            lax.fori_loop(1, n_d, step, 0)

    barrier = pltpu.get_barrier_semaphore()

    def greet(i, carry):
        t = lax.rem(me_d + i, n_d)
        pl.semaphore_signal(barrier, inc=1, device_id=(me_q, t), device_id_type=MESH)
        return carry

    peer_loop(greet)
    for dq in range(1, n_q):
        for k in range(grp):
            pl.semaphore_signal(
                barrier,
                inc=1,
                device_id=(lax.rem(me_q + dq, n_q), far * grp + k),
                device_id_type=MESH,
            )
    greeted = n_d - 1 + (n_q - 1) * grp
    loads = [
        pltpu.make_async_copy(src, dst, load_sem.at[k])
        for k, (src, dst) in enumerate(zip(hbm, local))
    ]
    for load in loads[::-1]:
        load.start()
    for load in loads[::-1]:
        load.wait()

    def exchange_start(phase, src, dst, size):
        def go(i, carry):
            peer = lax.rem(me_d + i, n_d)
            if size is None:
                s, d = src.at[peer], dst.at[me_d]
            else:
                s = src.at[pl.ds(pl.multiple_of(peer * size, size), size)]
                d = dst.at[pl.ds(pl.multiple_of(me_d * size, size), size)]
            pltpu.make_async_remote_copy(
                src_ref=s,
                dst_ref=d,
                send_sem=xsend.at[phase],
                recv_sem=xrecv.at[phase],
                device_id=(me_q, peer),
                device_id_type=MESH,
            ).start()
            return carry

        peer_loop(go)
        if size is None:
            dst[me_d] = src[me_d]
        else:
            own = pl.ds(pl.multiple_of(me_d * size, size), size)
            dst[own, :] = src[own, :]

    def exchange_wait(phase, src, dst, size):
        some = pl.ds(0, (n_d - 1) * (size or 1))
        pltpu.make_async_remote_copy(
            src_ref=src.at[some],
            dst_ref=dst.at[some],
            send_sem=xsend.at[phase],
            recv_sem=xrecv.at[phase],
            device_id=(me_q, lax.rem(me_d + 1, n_d)),
            device_id_type=MESH,
        ).wait()

    def near_device(t):
        return lax.div(t, grp), far * grp + lax.rem(t, grp)

    def all_copy(layer, stage, src, dst, device):
        return pltpu.make_async_remote_copy(
            src_ref=src,
            dst_ref=dst,
            send_sem=asend.at[layer, stage],
            recv_sem=arecv.at[layer, stage],
            device_id=device,
            device_id_type=MESH,
        )

    def scatter_start(layer):
        def go(j, carry):
            t = lax.rem(me_n + j, n_near)
            all_copy(layer, 0, red_src.at[layer, t], red_in.at[layer, me_n], near_device(t)).start()
            return carry

        loop(1, n_near, go)

    def far_start(layer):
        some = pl.ds(0, n_near - 1)
        all_copy(
            layer, 0, red_src.at[layer, some], red_in.at[layer, some], near_device(lax.rem(me_n + 1, n_near))
        ).wait()
        red_in[layer, me_n] = red_src[layer, me_n]
        red_z[layer, far] = jnp.sum(red_in[layer].astype(F32), axis=0).astype(BF16)

        def go(j, carry):
            t = lax.rem(far + j, n_far)
            all_copy(layer, 1, red_z.at[layer, far], red_z.at[layer, far], (me_q, t * grp + near)).start()
            return carry

        loop(1, n_far, go)

    def gather_start(layer):
        if n_far > 1:
            some = pl.ds(0, n_far - 1)
            all_copy(
                layer,
                1,
                red_z.at[layer, some],
                red_z.at[layer, some],
                (me_q, lax.rem(far + 1, n_far) * grp + near),
            ).wait()
        red_all[layer, me_n] = jnp.sum(red_z[layer].astype(F32), axis=0).astype(BF16)

        def go(j, carry):
            t = lax.rem(me_n + j, n_near)
            all_copy(layer, 2, red_all.at[layer, me_n], red_all.at[layer, me_n], near_device(t)).start()
            return carry

        loop(1, n_near, go)

    def gather_wait(layer):
        some = pl.ds(0, n_near - 1)
        all_copy(
            layer, 2, red_all.at[layer, some], red_all.at[layer, some], near_device(lax.rem(me_n + 1, n_near))
        ).wait()

    def pack(layer, rg, wg):
        parts = [rg, wg]
        left = width - rel_rows - feat
        if left:
            parts.append(jnp.zeros((feat, left), F32))
        whole = jnp.concatenate(parts, axis=1)
        red_src[layer] = whole.reshape(n_near, feat // n_near, width).astype(BF16)

    def unpack(layer):
        summed = red_all[layer].astype(F32).reshape(feat, width)
        grel_ref[layer] = summed[:, :rel_count] * scale_r
        gw_ref[layer] = summed[:, rel_rows : rel_rows + feat] * scale_w

    per = 128 // send
    spread = jnp.concatenate([gs_ref[...]] * per, axis=1)
    for p in range(n_d):
        gs_x[p] = spread[p : p + 1, :]

    onehot_into(vt, ein_ref[1:2, :], 0, 64)
    onehot_into(vt, ebd_ref[1:2, :], e_in, 64)
    pl.semaphore_wait(barrier, greeted)
    exchange_start(0, gs_x, req, None)
    onehot_into(st_in, ein_ref[0:1, :], 0, 64)
    onehot_into(st_bd, ebd_ref[0:1, :], 0, 64)

    slots = bnd_ref.shape[1]
    own_ids = lax.broadcasted_iota(jnp.int32, (rows, slots), 0)
    row_of32 = jnp.where(own_ids == bnd_ref[...], 1.0, 0.0)
    row_of = row_of32.astype(BF16)
    published = dot_nn(row_of32.T.astype(BF16), h_ref[...]).astype(BF16)

    exchange_wait(0, gs_x, req, None)
    lane_group = lax.broadcasted_iota(jnp.int32, (1, 128), 1) // send
    wanted = []
    for j in range(n_d // per):
        vec = jnp.zeros((1, 128), jnp.int32)
        for k in range(per):
            vec = jnp.where(lane_group == k, req[j * per + k, 0:1, :], vec)
        wanted.append(vec)
    wanted = jnp.concatenate(wanted, axis=1)
    slot_ids = lax.broadcasted_iota(jnp.int32, (slots, n_d * send), 0)
    slot_of32 = jnp.where(slot_ids == wanted, 1.0, 0.0)
    slot_of_t = slot_of32.T.astype(BF16)
    out1[...] = dot_nn(slot_of_t, published).astype(BF16)
    exchange_start(1, out1, ghost1, send)

    onehot_into(rt, ein_ref[2:3, :], 0, 32)
    onehot_into(rt, ebd_ref[2:3, :], e_in, 32)
    relt[...] = jnp.zeros_like(relt)
    relt[pl.ds(0, feat), pl.ds(0, rel_count)] = r1_ref[...]
    relt[pl.ds(feat, feat), pl.ds(0, rel_count)] = r2_ref[...]
    rel_e[...] = dot_nn(relt[...], rt[...]).astype(BF16)
    pick_t = dot_nn(row_of, slot_of32.astype(BF16)).astype(BF16)
    pick = dot_nt(slot_of_t, row_of).astype(BF16)

    row_ids = lax.broadcasted_iota(jnp.int32, (feat, rows), 1) + me_d * rows
    lane_rel = lax.broadcasted_iota(jnp.int32, (feat, rel_count), 1)
    qtab = qe_ref[...].astype(F32)
    boost_parts = []
    for q in range(queries):
        vec = jnp.sum(jnp.where(lane_rel == qrel_ref[q], qtab, 0.0), axis=1, keepdims=True)
        boost_parts.append(jnp.where(row_ids == qhead_ref[q], vec, 0.0))
    boost = jnp.concatenate(boost_parts, axis=0)

    h32 = h_ref[...].astype(F32)
    h_t32 = h32.T
    h_t = h_t32.astype(BF16)

    def rel_tile(layer, lo, count):
        part = rel_e[pl.ds(layer * feat, feat), pl.ds(lo, count)].astype(F32)
        return jnp.concatenate([part] * queries, axis=0)

    def aggregate(layer, table_t, onehot, save, lo, count):
        sourced = dot_nn(table_t, onehot[...])
        save[:, pl.ds(lo, count)] = sourced.astype(BF16)
        message = split_hi_lo(sourced * rel_tile(layer, lo, count), 0)
        both = dot_nt(message, vt[:, pl.ds(lo, count)])
        return both[:wide] + both[wide:]

    def normalise(summed, w_ref):
        summed_b = summed.astype(BF16)
        normed, rstds = [], []
        for q in range(queries):
            mixed = lax.dot_general(
                w_ref[...],
                summed_b[q * feat : (q + 1) * feat],
                (((0,), (0,)), ((), ())),
                preferred_element_type=F32,
            )
            center = mixed - jnp.mean(mixed, axis=0, keepdims=True)
            rstd = lax.rsqrt(jnp.mean(center * center, axis=0, keepdims=True) + 1e-05)
            normed.append(center * rstd)
            rstds.append(rstd)
        return summed_b, normed, rstds

    def back_layer(up_t, normed, rstds, w_ref):
        dmixes, dsum = [], []
        for q in range(queries):
            y = normed[q]
            sig = jax.nn.sigmoid(y)
            dact = up_t[q * feat : (q + 1) * feat] * sig * (1.0 + y * (1.0 - sig))
            dmix = rstds[q] * (
                dact
                - jnp.mean(dact, axis=0, keepdims=True)
                - y * jnp.mean(dact * y, axis=0, keepdims=True)
            )
            dmix_b = dmix.astype(BF16)
            dmixes.append(dmix_b)
            dsum.append(dot_nn(w_ref[...], dmix_b).astype(BF16))
        return dmixes, jnp.concatenate(dsum, axis=0)

    def weight_grad(summed_b, dmixes):
        wgrad = jnp.zeros((feat, feat), F32)
        for q in range(queries):
            wgrad = wgrad + dot_nt(summed_b[q * feat : (q + 1) * feat], dmixes[q])
        return wgrad

    def rel_grad(downs, save):
        tots = []
        lo = 0
        for down in downs:
            count = down.shape[1]
            prod = down * save[:, pl.ds(lo, count)].astype(F32)
            tot = prod[:feat]
            for q in range(1, queries):
                tot = tot + prod[q * feat : (q + 1) * feat]
            tots.append(tot.astype(BF16))
            lo += count
        return dot_nt(jnp.concatenate(tots, axis=1), rt[pl.ds(0, rel_rows), :])

    def table_grad(layer, down, onehot, lo, count):
        message = (down * rel_tile(layer, lo, count)).astype(BF16)
        return dot_nt(onehot[...], message)

    def give_back(ret_in):
        return dot_nn(pick_t, ret_in[...])

    sum1 = aggregate(0, h_t, st_in, x1, 0, e_in) + boost
    exchange_wait(1, out1, ghost1, send)
    sum1 = sum1 + aggregate(0, ghost1[...].astype(F32).T.astype(BF16), st_bd, x1, e_in, e_bd)
    sum1_b, norm1, rstd1 = normalise(sum1, w1_ref)
    h2_t = (
        jnp.concatenate([y * jax.nn.sigmoid(y) for y in norm1], axis=0) + h_t32
    ).astype(BF16)

    out2[...] = dot_nt(pick, h2_t).astype(BF16)
    exchange_start(2, out2, ghost2, send)
    sum2 = aggregate(1, h2_t, st_in, x2, 0, e_in) + boost
    exchange_wait(2, out2, ghost2, send)
    sum2 = sum2 + aggregate(1, ghost2[...].astype(F32).T.astype(BF16), st_bd, x2, e_in, e_bd)
    sum2_b, norm2, rstd2 = normalise(sum2, w2_ref)

    cot32 = cot_ref[...].astype(F32)
    dmix2, dsum2 = back_layer(cot32.T, norm2, rstd2, w2_ref)
    down2_bd = dot_nn(dsum2, vt[:, pl.ds(e_in, e_bd)])
    ret_out2[...] = table_grad(1, down2_bd, st_bd, e_in, e_bd).astype(BF16)
    exchange_start(3, ret_out2, ret_in2, send)
    down2_in = dot_nn(dsum2, vt[:, pl.ds(0, e_in)])
    pack(1, rel_grad((down2_in, down2_bd), x2), weight_grad(sum2_b, dmix2))
    scatter_start(1)
    mid = cot32 + table_grad(1, down2_in, st_in, 0, e_in)
    exchange_wait(3, ret_out2, ret_in2, send)
    mid = mid + give_back(ret_in2)

    dmix1, dsum1 = back_layer(mid.T, norm1, rstd1, w1_ref)
    down1_in = dot_nn(dsum1, vt[:, pl.ds(0, e_in)])
    down1_bd = dot_nn(dsum1, vt[:, pl.ds(e_in, e_bd)])
    pack(0, rel_grad((down1_in, down1_bd), x1), weight_grad(sum1_b, dmix1))
    scatter_start(0)
    far_start(1)
    ret_out1[...] = table_grad(0, down1_bd, st_bd, e_in, e_bd).astype(BF16)
    exchange_start(4, ret_out1, ret_in1, send)
    base = mid + table_grad(0, down1_in, st_in, 0, e_in)
    far_start(0)
    gather_start(1)
    exchange_wait(4, ret_out1, ret_in1, send)
    gin_ref[...] = base + give_back(ret_in1)
    gather_start(0)
    gather_wait(1)
    unpack(1)
    gather_wait(0)
    unpack(0)


def write_out(*refs):
    half = (len(refs) - 1) // 2
    copies = [
        pltpu.make_async_copy(src, dst, refs[-1].at[k])
        for k, (src, dst) in enumerate(zip(refs[:half], refs[half : 2 * half]))
    ]
    for copy in copies:
        copy.start()
    for copy in copies:
        copy.wait()


def body(
    h_in,
    cotangent,
    w_one,
    w_two,
    rel_one,
    rel_two,
    query_emb,
    q_head,
    q_rel,
    bnd_rows,
    ghost_slots,
    edges_in,
    edges_bd,
):
    rows, wide = h_in.shape
    feat = w_one.shape[0]
    queries = wide // feat
    rel_count = rel_one.shape[0]
    n_d = lax.axis_size("dom")
    n_q = lax.axis_size("query")
    send = ghost_slots.shape[1]
    ghosts = n_d * send
    e_in, e_bd = edges_in.shape[1], edges_bd.shape[1]
    edges = e_in + e_bd
    rel_pad = -(-(rel_count + 1) // 128) * 128
    rel_rows = -(-(rel_count + 1) // 16) * 16
    width = -(-(rel_rows + feat) // 128) * 128
    grp = max(1, 8 // n_q)
    n_near, n_far = n_q * grp, n_d // grp
    part = feat // n_near
    scale_w = 1.0 / math.sqrt(rows * n_d * queries * n_q)
    scale_r = math.sqrt(rel_count / (n_d * edges * queries * n_q))

    args = (
        h_in,
        cotangent,
        w_one,
        w_two,
        rel_one.T,
        rel_two.T,
        query_emb.T,
        q_head,
        q_rel,
        bnd_rows[None, :],
        ghost_slots,
        edges_in,
        edges_bd,
    )
    spaces = [pltpu.VMEM] * 7 + [pltpu.SMEM] * 2 + [pltpu.VMEM] * 4

    vmem = pl.BlockSpec(memory_space=pltpu.VMEM)
    dma = pltpu.SemaphoreType.DMA
    shapes = (
        jax.ShapeDtypeStruct((rows, wide), F32),
        jax.ShapeDtypeStruct((2, feat, feat), F32),
        jax.ShapeDtypeStruct((2, feat, rel_count), F32),
    )
    results = pl.pallas_call(
        functools.partial(kernel, n_q, n_d, grp, scale_w, scale_r, rel_count, rel_rows),
        out_shape=tuple(pltpu.VMEM(s.shape, s.dtype) for s in shapes),
        in_specs=[pl.BlockSpec(memory_space=pltpu.HBM)] * len(args),
        out_specs=(vmem, vmem, vmem),
        scratch_shapes=[
            *(space(a.shape, a.dtype) for a, space in zip(args, spaces)),
            pltpu.VMEM((2 * feat, rel_pad), BF16),
            pltpu.VMEM((n_d, 1, 128), jnp.int32),
            pltpu.VMEM((rel_pad, edges), BF16),
            pltpu.VMEM((rows, edges), BF16),
            pltpu.VMEM((rows, e_in), BF16),
            pltpu.VMEM((ghosts, e_bd), BF16),
            pltpu.VMEM((2 * feat, edges), BF16),
            pltpu.VMEM((wide, edges), BF16),
            pltpu.VMEM((wide, edges), BF16),
            pltpu.VMEM((n_d, 1, 128), jnp.int32),
            pltpu.VMEM((ghosts, wide), BF16),
            pltpu.VMEM((ghosts, wide), BF16),
            pltpu.VMEM((ghosts, wide), BF16),
            pltpu.VMEM((ghosts, wide), BF16),
            pltpu.VMEM((ghosts, wide), BF16),
            pltpu.VMEM((ghosts, wide), BF16),
            pltpu.VMEM((ghosts, wide), BF16),
            pltpu.VMEM((ghosts, wide), BF16),
            pltpu.VMEM((2, n_near, part, width), BF16),
            pltpu.VMEM((2, n_near, part, width), BF16),
            pltpu.VMEM((2, n_far, part, width), BF16),
            pltpu.VMEM((2, n_near, part, width), BF16),
            dma((5,)),
            dma((5,)),
            dma((2, 3)),
            dma((2, 3)),
            dma((len(args),)),
        ],
        compiler_params=pltpu.CompilerParams(
            collective_id=0, has_side_effects=True, vmem_limit_bytes=33554432
        ),
    )(*(pltpu.with_memory_space_constraint(a, pltpu.HBM) for a in args))
    grad_in, grad_w, grad_rel_t = pl.pallas_call(
        write_out,
        out_shape=shapes,
        in_specs=[vmem] * 3,
        out_specs=[pl.BlockSpec(memory_space=pltpu.HBM)] * 3,
        scratch_shapes=[dma((3,))],
        compiler_params=pltpu.CompilerParams(vmem_limit_bytes=16777216),
    )(*results)
    return grad_in, grad_w, jnp.swapaxes(grad_rel_t, 1, 2)


def solution(mesh):
    return jax.shard_map(
        body,
        mesh=mesh,
        in_specs=(
            P("dom", "query"),
            P("dom", "query"),
            P(),
            P(),
            P(),
            P(),
            P(),
            P("query"),
            P("query"),
            P("dom"),
            P("dom", None),
            P(None, "dom"),
            P(None, "dom"),
        ),
        out_specs=(P("dom", "query"), P(), P()),
        check_vma=False,
    )
```

```python
import functools
import math

import jax
import jax.numpy as jnp
from jax import lax
from jax.experimental import pallas as pl
from jax.experimental.pallas import tpu as pltpu
from jax.sharding import PartitionSpec as P

MESH = pl.DeviceIdType.MESH
F32 = jnp.float32
BF16 = jnp.bfloat16


def dot_nn(a, b):
    return lax.dot_general(a, b, (((1,), (0,)), ((), ())), preferred_element_type=F32)


def dot_nt(a, b):
    return lax.dot_general(a, b, (((1,), (1,)), ((), ())), preferred_element_type=F32)


def split_hi_lo(x, axis):
    hi = x.astype(BF16)
    lo = (x - hi.astype(F32)).astype(BF16)
    return jnp.concatenate([hi, lo], axis=axis)


def onehot_into(dest, ids, col0, block):
    rows = dest.shape[0]
    count = ids.shape[1]

    def fill(i, carry):
        base = pl.multiple_of(i * block, block)
        row_ids = lax.broadcasted_iota(jnp.int32, (block, count), 0) + base
        dest[pl.ds(base, block), pl.ds(col0, count)] = jnp.where(row_ids == ids, 1.0, 0.0).astype(BF16)
        return carry

    lax.fori_loop(0, rows // block, fill, 0)


def loop(low, high, step):
    if high - low <= 32:
        for i in range(low, high):
            step(i, 0)
    else:
        lax.fori_loop(low, high, step, 0)


def div(a, b):
    return a // b if isinstance(a, int) else lax.div(a, b)


def rem(a, b):
    return a % b if isinstance(a, int) else lax.rem(a, b)


def aligned(a, b):
    return a if isinstance(a, int) else pl.multiple_of(a, b)


def kernel(
    n_q,
    n_d,
    grp,
    scale_w,
    scale_r,
    rel_count,
    rel_rows,
    *refs,
):
    n_in = 13
    hbm = refs[:n_in]
    gin_ref, gw_ref, grel_ref = refs[n_in : n_in + 3]
    local = refs[n_in + 3 : 2 * n_in + 3]
    (
        h_ref, cot_ref, w1_ref, w2_ref, r1_ref, r2_ref, qe_ref, qhead_ref, qrel_ref, bnd_ref, gs_ref, ein_ref, ebd_ref,
    ) = local
    (
    relt,
    gs_x,
    rt,
    vt,
    st_in,
    st_bd,
    rel_e,
    x1,
    x2,
    req,
    out1,
    ghost1,
    out2,
    ghost2,
    ret_out2,
    ret_in2,
    ret_out1,
    ret_in1,
    cot_t,
    slope1,
    red_src,
    red_in,
    red_z,
    red_all,
    xsend,
    xrecv,
    asend,
    arecv,
    load_sem,
    ) = refs[2 * n_in + 3 :]
    me_d = lax.axis_index("dom")
    me_q = lax.axis_index("query")
    n_far = n_d // grp
    n_near = n_q * grp
    far = lax.div(me_d, grp)
    near = lax.rem(me_d, grp)
    me_n = me_q * grp + near
    feat = w1_ref.shape[0]
    rows, wide = h_ref.shape
    queries = wide // feat
    send = ghost1.shape[0] // n_d
    e_in = ein_ref.shape[1]
    e_bd = ebd_ref.shape[1]
    width = red_src.shape[3]

    def peer_loop(step):
        if n_d <= 32:
            order = sorted(range(1, n_d), key=lambda i: -min(i // grp, n_far - i // grp))
            for i in order:
                step(i, 0)
        else:
            lax.fori_loop(1, n_d, step, 0)

    barrier = pltpu.get_barrier_semaphore()

    def greet(i, carry):
        t = lax.rem(me_d + i, n_d)
        pl.semaphore_signal(barrier, inc=1, device_id=(me_q, t), device_id_type=MESH)
        return carry

    peer_loop(greet)
    for dq in range(1, n_q):
        for k in range(grp):
            pl.semaphore_signal(
                barrier,
                inc=1,
                device_id=(lax.rem(me_q + dq, n_q), far * grp + k),
                device_id_type=MESH,
            )
    greeted = n_d - 1 + (n_q - 1) * grp
    loads = [
        pltpu.make_async_copy(src, dst, load_sem.at[k])
        for k, (src, dst) in enumerate(zip(hbm, local))
    ]
    for load in loads[::-1]:
        load.start()
    for load in loads[::-1]:
        load.wait()

    def exchange_start(phase, src, dst, size):
        def go(i, carry):
            peer = lax.rem(me_d + i, n_d)
            if size is None:
                s, d = src.at[peer], dst.at[me_d]
            else:
                s = src.at[pl.ds(pl.multiple_of(peer * size, size), size)]
                d = dst.at[pl.ds(pl.multiple_of(me_d * size, size), size)]
            pltpu.make_async_remote_copy(
                src_ref=s,
                dst_ref=d,
                send_sem=xsend.at[phase],
                recv_sem=xrecv.at[phase],
                device_id=(me_q, peer),
                device_id_type=MESH,
            ).start()
            return carry

        peer_loop(go)
        if size is None:
            dst[me_d] = src[me_d]
        else:
            own = pl.ds(pl.multiple_of(me_d * size, size), size)
            dst[own, :] = src[own, :]

    def exchange_wait(phase, src, dst, size):
        some = pl.ds(0, (n_d - 1) * (size or 1))
        pltpu.make_async_remote_copy(
            src_ref=src.at[some],
            dst_ref=dst.at[some],
            send_sem=xsend.at[phase],
            recv_sem=xrecv.at[phase],
            device_id=(me_q, lax.rem(me_d + 1, n_d)),
            device_id_type=MESH,
        ).wait()

    def near_device(t):
        return lax.div(t, grp), far * grp + lax.rem(t, grp)

    def all_copy(layer, stage, src, dst, device):
        return pltpu.make_async_remote_copy(
            src_ref=src,
            dst_ref=dst,
            send_sem=asend.at[layer, stage],
            recv_sem=arecv.at[layer, stage],
            device_id=device,
            device_id_type=MESH,
        )

    def scatter_start(layer):
        def go(j, carry):
            t = lax.rem(me_n + j, n_near)
            all_copy(layer, 0, red_src.at[layer, t], red_in.at[layer, me_n], near_device(t)).start()
            return carry

        loop(1, n_near, go)

    def far_start(layer):
        some = pl.ds(0, n_near - 1)
        all_copy(
            layer, 0, red_src.at[layer, some], red_in.at[layer, some], near_device(lax.rem(me_n + 1, n_near))
        ).wait()
        red_in[layer, me_n] = red_src[layer, me_n]
        red_z[layer, far] = jnp.sum(red_in[layer].astype(F32), axis=0).astype(BF16)

        def go(j, carry):
            t = lax.rem(far + j, n_far)
            all_copy(layer, 1, red_z.at[layer, far], red_z.at[layer, far], (me_q, t * grp + near)).start()
            return carry

        loop(1, n_far, go)

    def gather_start(layer):
        if n_far > 1:
            some = pl.ds(0, n_far - 1)
            all_copy(
                layer,
                1,
                red_z.at[layer, some],
                red_z.at[layer, some],
                (me_q, lax.rem(far + 1, n_far) * grp + near),
            ).wait()
        red_all[layer, me_n] = jnp.sum(red_z[layer].astype(F32), axis=0).astype(BF16)

        def go(j, carry):
            t = lax.rem(me_n + j, n_near)
            all_copy(layer, 2, red_all.at[layer, me_n], red_all.at[layer, me_n], near_device(t)).start()
            return carry

        loop(1, n_near, go)

    def gather_wait(layer):
        some = pl.ds(0, n_near - 1)
        all_copy(
            layer, 2, red_all.at[layer, some], red_all.at[layer, some], near_device(lax.rem(me_n + 1, n_near))
        ).wait()

    def pack(layer, rg, wg):
        parts = [rg, wg]
        left = width - rel_rows - feat
        if left:
            parts.append(jnp.zeros((feat, left), F32))
        whole = jnp.concatenate(parts, axis=1)
        red_src[layer] = whole.reshape(n_near, feat // n_near, width).astype(BF16)

    def unpack(layer):
        summed = red_all[layer].astype(F32).reshape(feat, width)
        grel_ref[layer] = summed[:, :rel_count] * scale_r
        gw_ref[layer] = summed[:, rel_rows : rel_rows + feat] * scale_w

    per = 128 // send
    spread = jnp.concatenate([gs_ref[...]] * per, axis=1)
    for p in range(n_d):
        gs_x[p] = spread[p : p + 1, :]

    onehot_into(vt, ein_ref[1:2, :], 0, 64)
    onehot_into(vt, ebd_ref[1:2, :], e_in, 64)
    pl.semaphore_wait(barrier, greeted)
    exchange_start(0, gs_x, req, None)
    onehot_into(st_in, ein_ref[0:1, :], 0, 64)
    onehot_into(st_bd, ebd_ref[0:1, :], 0, 64)

    slots = bnd_ref.shape[1]
    own_ids = lax.broadcasted_iota(jnp.int32, (rows, slots), 0)
    row_of32 = jnp.where(own_ids == bnd_ref[...], 1.0, 0.0)
    row_of = row_of32.astype(BF16)
    published = dot_nn(row_of32.T.astype(BF16), h_ref[...]).astype(BF16)

    exchange_wait(0, gs_x, req, None)
    lane_group = lax.broadcasted_iota(jnp.int32, (1, 128), 1) // send
    wanted = []
    for j in range(n_d // per):
        vec = jnp.zeros((1, 128), jnp.int32)
        for k in range(per):
            vec = jnp.where(lane_group == k, req[j * per + k, 0:1, :], vec)
        wanted.append(vec)
    wanted = jnp.concatenate(wanted, axis=1)
    slot_ids = lax.broadcasted_iota(jnp.int32, (slots, n_d * send), 0)
    slot_of32 = jnp.where(slot_ids == wanted, 1.0, 0.0)
    slot_of_t = slot_of32.T.astype(BF16)
    out1[...] = dot_nn(slot_of_t, published).astype(BF16)
    exchange_start(1, out1, ghost1, send)

    onehot_into(rt, ein_ref[2:3, :], 0, 32)
    onehot_into(rt, ebd_ref[2:3, :], e_in, 32)
    relt[...] = jnp.zeros_like(relt)
    relt[pl.ds(0, feat), pl.ds(0, rel_count)] = r1_ref[...]
    relt[pl.ds(feat, feat), pl.ds(0, rel_count)] = r2_ref[...]
    rel_e[...] = dot_nn(relt[...], rt[...]).astype(BF16)
    pick_t = dot_nn(row_of, slot_of32.astype(BF16)).astype(BF16)
    pick = dot_nt(slot_of_t, row_of).astype(BF16)

    row_ids = lax.broadcasted_iota(jnp.int32, (feat, rows), 1) + me_d * rows
    lane_rel = lax.broadcasted_iota(jnp.int32, (feat, rel_count), 1)
    qtab = qe_ref[...].astype(F32)
    boost_parts = []
    for q in range(queries):
        vec = jnp.sum(jnp.where(lane_rel == qrel_ref[q], qtab, 0.0), axis=1, keepdims=True)
        boost_parts.append(jnp.where(row_ids == qhead_ref[q], vec, 0.0))
    boost = jnp.concatenate(boost_parts, axis=0)

    h32 = h_ref[...].astype(F32)
    h_t32 = h32.T
    h_t = h_t32.astype(BF16)

    def rel_tile(layer, lo, count):
        part = rel_e[pl.ds(layer * feat, feat), pl.ds(lo, count)].astype(F32)
        return jnp.concatenate([part] * queries, axis=0)

    def aggregate(layer, table_t, onehot, save, lo, count):
        sourced = dot_nn(table_t, onehot[...])
        save[:, pl.ds(lo, count)] = sourced.astype(BF16)
        message = split_hi_lo(sourced * rel_tile(layer, lo, count), 0)
        both = dot_nt(message, vt[:, pl.ds(lo, count)])
        return both[:wide] + both[wide:]

    def normalise(summed, w_ref):
        summed_b = summed.astype(BF16)
        normed, rstds = [], []
        for q in range(queries):
            mixed = lax.dot_general(
                w_ref[...],
                summed_b[q * feat : (q + 1) * feat],
                (((0,), (0,)), ((), ())),
                preferred_element_type=F32,
            )
            center = mixed - jnp.mean(mixed, axis=0, keepdims=True)
            rstd = lax.rsqrt(jnp.mean(center * center, axis=0, keepdims=True) + 1e-05)
            normed.append(center * rstd)
            rstds.append(rstd)
        return summed_b, normed, rstds

    def silu_slope(y):
        sig = jax.nn.sigmoid(y)
        return sig * (1.0 + y * (1.0 - sig))

    def back_layer(up_t, slopes, normed, rstds, w_ref):
        dmixes, dsum = [], []
        for q in range(queries):
            y = normed[q]
            dact = up_t[q * feat : (q + 1) * feat] * slopes[q]
            dmix = rstds[q] * (
                dact
                - jnp.mean(dact, axis=0, keepdims=True)
                - y * jnp.mean(dact * y, axis=0, keepdims=True)
            )
            dmix_b = dmix.astype(BF16)
            dmixes.append(dmix_b)
            dsum.append(dot_nn(w_ref[...], dmix_b).astype(BF16))
        return dmixes, jnp.concatenate(dsum, axis=0)

    def weight_grad(summed_b, dmixes):
        wgrad = jnp.zeros((feat, feat), F32)
        for q in range(queries):
            wgrad = wgrad + dot_nt(summed_b[q * feat : (q + 1) * feat], dmixes[q])
        return wgrad

    def rel_grad(downs, save):
        tots = []
        lo = 0
        for down in downs:
            count = down.shape[1]
            prod = down * save[:, pl.ds(lo, count)].astype(F32)
            tot = prod[:feat]
            for q in range(1, queries):
                tot = tot + prod[q * feat : (q + 1) * feat]
            tots.append(tot.astype(BF16))
            lo += count
        return dot_nt(jnp.concatenate(tots, axis=1), rt[pl.ds(0, rel_rows), :])

    def table_grad(layer, down, onehot, lo, count):
        part = rel_e[pl.ds(layer * feat, feat), pl.ds(lo, count)]
        message = down.astype(BF16) * jnp.concatenate([part] * queries, axis=0)
        return dot_nt(onehot[...], message)

    def give_back(ret_in):
        return dot_nn(pick_t, ret_in[...])

    sum1 = aggregate(0, h_t, st_in, x1, 0, e_in) + boost
    exchange_wait(1, out1, ghost1, send)
    sum1 = sum1 + aggregate(0, ghost1[...].astype(F32).T.astype(BF16), st_bd, x1, e_in, e_bd)
    sum1_b, norm1, rstd1 = normalise(sum1, w1_ref)
    h2_t = (
        jnp.concatenate([y * jax.nn.sigmoid(y) for y in norm1], axis=0) + h_t32
    ).astype(BF16)

    out2[...] = dot_nt(pick, h2_t).astype(BF16)
    exchange_start(2, out2, ghost2, send)
    sum2 = aggregate(1, h2_t, st_in, x2, 0, e_in) + boost
    cot32 = cot_ref[...].astype(F32)
    cot_t[...] = cot32.T
    for q in range(queries):
        slope1[pl.ds(q * feat, feat), :] = silu_slope(norm1[q])
    exchange_wait(2, out2, ghost2, send)
    sum2 = sum2 + aggregate(1, ghost2[...].astype(F32).T.astype(BF16), st_bd, x2, e_in, e_bd)
    sum2_b, norm2, rstd2 = normalise(sum2, w2_ref)

    dmix2, dsum2 = back_layer(cot_t[...], [silu_slope(y) for y in norm2], norm2, rstd2, w2_ref)
    down2_bd = dot_nn(dsum2, vt[:, pl.ds(e_in, e_bd)])
    ret_out2[...] = table_grad(1, down2_bd, st_bd, e_in, e_bd).astype(BF16)
    exchange_start(3, ret_out2, ret_in2, send)
    down2_in = dot_nn(dsum2, vt[:, pl.ds(0, e_in)])
    pack(1, rel_grad((down2_in, down2_bd), x2), weight_grad(sum2_b, dmix2))
    scatter_start(1)
    mid = cot32 + table_grad(1, down2_in, st_in, 0, e_in)
    exchange_wait(3, ret_out2, ret_in2, send)
    mid = mid + give_back(ret_in2)

    slopes1 = [slope1[pl.ds(q * feat, feat), :] for q in range(queries)]
    dmix1, dsum1 = back_layer(mid.T, slopes1, norm1, rstd1, w1_ref)
    down1_in = dot_nn(dsum1, vt[:, pl.ds(0, e_in)])
    down1_bd = dot_nn(dsum1, vt[:, pl.ds(e_in, e_bd)])
    pack(0, rel_grad((down1_in, down1_bd), x1), weight_grad(sum1_b, dmix1))
    scatter_start(0)
    far_start(1)
    ret_out1[...] = table_grad(0, down1_bd, st_bd, e_in, e_bd).astype(BF16)
    exchange_start(4, ret_out1, ret_in1, send)
    base = mid + table_grad(0, down1_in, st_in, 0, e_in)
    far_start(0)
    gather_start(1)
    exchange_wait(4, ret_out1, ret_in1, send)
    gin_ref[...] = base + give_back(ret_in1)
    gather_start(0)
    gather_wait(1)
    unpack(1)
    gather_wait(0)
    unpack(0)


def write_out(*refs):
    half = (len(refs) - 1) // 2
    copies = [
        pltpu.make_async_copy(src, dst, refs[-1].at[k])
        for k, (src, dst) in enumerate(zip(refs[:half], refs[half : 2 * half]))
    ]
    for copy in copies:
        copy.start()
    for copy in copies:
        copy.wait()


def body(
    h_in,
    cotangent,
    w_one,
    w_two,
    rel_one,
    rel_two,
    query_emb,
    q_head,
    q_rel,
    bnd_rows,
    ghost_slots,
    edges_in,
    edges_bd,
):
    rows, wide = h_in.shape
    feat = w_one.shape[0]
    queries = wide // feat
    rel_count = rel_one.shape[0]
    n_d = lax.axis_size("dom")
    n_q = lax.axis_size("query")
    send = ghost_slots.shape[1]
    ghosts = n_d * send
    e_in, e_bd = edges_in.shape[1], edges_bd.shape[1]
    edges = e_in + e_bd
    rel_pad = -(-(rel_count + 1) // 128) * 128
    rel_rows = -(-(rel_count + 1) // 16) * 16
    width = -(-(rel_rows + feat) // 128) * 128
    grp = max(1, 8 // n_q)
    n_near, n_far = n_q * grp, n_d // grp
    part = feat // n_near
    scale_w = 1.0 / math.sqrt(rows * n_d * queries * n_q)
    scale_r = math.sqrt(rel_count / (n_d * edges * queries * n_q))

    args = (
        h_in,
        cotangent,
        w_one,
        w_two,
        rel_one.T,
        rel_two.T,
        query_emb.T,
        q_head,
        q_rel,
        bnd_rows[None, :],
        ghost_slots,
        edges_in,
        edges_bd,
    )
    spaces = [pltpu.VMEM] * 7 + [pltpu.SMEM] * 2 + [pltpu.VMEM] * 4

    vmem = pl.BlockSpec(memory_space=pltpu.VMEM)
    dma = pltpu.SemaphoreType.DMA
    shapes = (
        jax.ShapeDtypeStruct((rows, wide), F32),
        jax.ShapeDtypeStruct((2, feat, feat), F32),
        jax.ShapeDtypeStruct((2, feat, rel_count), F32),
    )
    results = pl.pallas_call(
        functools.partial(kernel, n_q, n_d, grp, scale_w, scale_r, rel_count, rel_rows),
        out_shape=tuple(pltpu.VMEM(s.shape, s.dtype) for s in shapes),
        in_specs=[pl.BlockSpec(memory_space=pltpu.HBM)] * len(args),
        out_specs=(vmem, vmem, vmem),
        scratch_shapes=[
            *(space(a.shape, a.dtype) for a, space in zip(args, spaces)),
            pltpu.VMEM((2 * feat, rel_pad), BF16),
            pltpu.VMEM((n_d, 1, 128), jnp.int32),
            pltpu.VMEM((rel_pad, edges), BF16),
            pltpu.VMEM((rows, edges), BF16),
            pltpu.VMEM((rows, e_in), BF16),
            pltpu.VMEM((ghosts, e_bd), BF16),
            pltpu.VMEM((2 * feat, edges), BF16),
            pltpu.VMEM((wide, edges), BF16),
            pltpu.VMEM((wide, edges), BF16),
            pltpu.VMEM((n_d, 1, 128), jnp.int32),
            pltpu.VMEM((ghosts, wide), BF16),
            pltpu.VMEM((ghosts, wide), BF16),
            pltpu.VMEM((ghosts, wide), BF16),
            pltpu.VMEM((ghosts, wide), BF16),
            pltpu.VMEM((ghosts, wide), BF16),
            pltpu.VMEM((ghosts, wide), BF16),
            pltpu.VMEM((ghosts, wide), BF16),
            pltpu.VMEM((ghosts, wide), BF16),
            pltpu.VMEM((wide, rows), F32),
            pltpu.VMEM((wide, rows), F32),
            pltpu.VMEM((2, n_near, part, width), BF16),
            pltpu.VMEM((2, n_near, part, width), BF16),
            pltpu.VMEM((2, n_far, part, width), BF16),
            pltpu.VMEM((2, n_near, part, width), BF16),
            dma((5,)),
            dma((5,)),
            dma((2, 3)),
            dma((2, 3)),
            dma((len(args),)),
        ],
        compiler_params=pltpu.CompilerParams(
            collective_id=0, has_side_effects=True, vmem_limit_bytes=33554432
        ),
    )(*(pltpu.with_memory_space_constraint(a, pltpu.HBM) for a in args))
    grad_in, grad_w, grad_rel_t = pl.pallas_call(
        write_out,
        out_shape=shapes,
        in_specs=[vmem] * 3,
        out_specs=[pl.BlockSpec(memory_space=pltpu.HBM)] * 3,
        scratch_shapes=[dma((3,))],
        compiler_params=pltpu.CompilerParams(vmem_limit_bytes=16777216),
    )(*results)
    return grad_in, grad_w, jnp.swapaxes(grad_rel_t, 1, 2)


def solution(mesh):
    return jax.shard_map(
        body,
        mesh=mesh,
        in_specs=(
            P("dom", "query"),
            P("dom", "query"),
            P(),
            P(),
            P(),
            P(),
            P(),
            P("query"),
            P("query"),
            P("dom"),
            P("dom", None),
            P(None, "dom"),
            P(None, "dom"),
        ),
        out_specs=(P("dom", "query"), P(), P()),
        check_vma=False,
    )
```

```python
import functools
import math

import jax
import jax.numpy as jnp
from jax import lax
from jax.experimental import pallas as pl
from jax.experimental.pallas import tpu as pltpu
from jax.sharding import PartitionSpec as P

MESH = pl.DeviceIdType.MESH
F32 = jnp.float32
BF16 = jnp.bfloat16


def dot_nn(a, b):
    return lax.dot_general(a, b, (((1,), (0,)), ((), ())), preferred_element_type=F32)


def dot_nt(a, b):
    return lax.dot_general(a, b, (((1,), (1,)), ((), ())), preferred_element_type=F32)


def split_hi_lo(x, axis):
    hi = x.astype(BF16)
    lo = (x - hi.astype(F32)).astype(BF16)
    return jnp.concatenate([hi, lo], axis=axis)


def onehot_into(dest, ids, col0, block):
    rows = dest.shape[0]
    count = ids.shape[1]

    def fill(i, carry):
        base = pl.multiple_of(i * block, block)
        row_ids = lax.broadcasted_iota(jnp.int32, (block, count), 0) + base
        dest[pl.ds(base, block), pl.ds(col0, count)] = jnp.where(row_ids == ids, 1.0, 0.0).astype(BF16)
        return carry

    lax.fori_loop(0, rows // block, fill, 0)


def loop(low, high, step):
    if high - low <= 32:
        for i in range(low, high):
            step(i, 0)
    else:
        lax.fori_loop(low, high, step, 0)


def div(a, b):
    return a // b if isinstance(a, int) else lax.div(a, b)


def rem(a, b):
    return a % b if isinstance(a, int) else lax.rem(a, b)


def aligned(a, b):
    return a if isinstance(a, int) else pl.multiple_of(a, b)


def kernel(
    n_q,
    n_d,
    grp,
    scale_w,
    scale_r,
    rel_count,
    rel_rows,
    *refs,
):
    n_in = 13
    hbm = refs[:n_in]
    gin_ref, gw_ref, grel_ref = refs[n_in : n_in + 3]
    local = refs[n_in + 3 : 2 * n_in + 3]
    (
        h_ref, cot_ref, w1_ref, w2_ref, r1_ref, r2_ref, qe_ref, qhead_ref, qrel_ref, bnd_ref, gs_ref, ein_ref, ebd_ref,
    ) = local
    (
    relt,
    gs_x,
    rt,
    vt,
    st_in,
    st_bd,
    rel_e,
    x1,
    x2,
    req,
    out1,
    ghost1,
    out2,
    ghost2,
    ret_out2,
    ret_in2,
    ret_out1,
    ret_in1,
    cot_t,
    slope1,
    red_src,
    red_in,
    red_z,
    red_all,
    xsend,
    xrecv,
    asend,
    arecv,
    load_sem,
    ) = refs[2 * n_in + 3 :]
    me_d = lax.axis_index("dom")
    me_q = lax.axis_index("query")
    n_far = n_d // grp
    n_near = n_q * grp
    far = lax.div(me_d, grp)
    near = lax.rem(me_d, grp)
    me_n = me_q * grp + near
    feat = w1_ref.shape[0]
    rows, wide = h_ref.shape
    queries = wide // feat
    send = ghost1.shape[0] // n_d
    e_in = ein_ref.shape[1]
    e_bd = ebd_ref.shape[1]
    width = red_src.shape[3]

    def peer_loop(step):
        if n_d <= 32:
            order = sorted(range(1, n_d), key=lambda i: -min(i // grp, n_far - i // grp))
            for i in order:
                step(i, 0)
        else:
            lax.fori_loop(1, n_d, step, 0)

    barrier = pltpu.get_barrier_semaphore()

    def greet(i, carry):
        t = lax.rem(me_d + i, n_d)
        pl.semaphore_signal(barrier, inc=1, device_id=(me_q, t), device_id_type=MESH)
        return carry

    peer_loop(greet)
    for dq in range(1, n_q):
        for k in range(grp):
            pl.semaphore_signal(
                barrier,
                inc=1,
                device_id=(lax.rem(me_q + dq, n_q), far * grp + k),
                device_id_type=MESH,
            )
    greeted = n_d - 1 + (n_q - 1) * grp
    loads = [
        pltpu.make_async_copy(src, dst, load_sem.at[k])
        for k, (src, dst) in enumerate(zip(hbm, local))
    ]
    for load in loads[::-1]:
        load.start()
    for load in loads[::-1]:
        load.wait()

    def exchange_start(phase, src, dst, size):
        def go(i, carry):
            peer = lax.rem(me_d + i, n_d)
            if size is None:
                s, d = src.at[peer], dst.at[me_d]
            else:
                s = src.at[pl.ds(pl.multiple_of(peer * size, size), size)]
                d = dst.at[pl.ds(pl.multiple_of(me_d * size, size), size)]
            pltpu.make_async_remote_copy(
                src_ref=s,
                dst_ref=d,
                send_sem=xsend.at[phase],
                recv_sem=xrecv.at[phase],
                device_id=(me_q, peer),
                device_id_type=MESH,
            ).start()
            return carry

        peer_loop(go)
        if size is None:
            dst[me_d] = src[me_d]
        else:
            own = pl.ds(pl.multiple_of(me_d * size, size), size)
            dst[own, :] = src[own, :]

    def exchange_wait(phase, src, dst, size):
        some = pl.ds(0, (n_d - 1) * (size or 1))
        pltpu.make_async_remote_copy(
            src_ref=src.at[some],
            dst_ref=dst.at[some],
            send_sem=xsend.at[phase],
            recv_sem=xrecv.at[phase],
            device_id=(me_q, lax.rem(me_d + 1, n_d)),
            device_id_type=MESH,
        ).wait()

    def near_device(t):
        return lax.div(t, grp), far * grp + lax.rem(t, grp)

    def all_copy(layer, stage, src, dst, device):
        return pltpu.make_async_remote_copy(
            src_ref=src,
            dst_ref=dst,
            send_sem=asend.at[layer, stage],
            recv_sem=arecv.at[layer, stage],
            device_id=device,
            device_id_type=MESH,
        )

    def scatter_start(layer):
        def go(j, carry):
            t = lax.rem(me_n + j, n_near)
            all_copy(layer, 0, red_src.at[layer, t], red_in.at[layer, me_n], near_device(t)).start()
            return carry

        loop(1, n_near, go)

    def far_start(layer):
        some = pl.ds(0, n_near - 1)
        all_copy(
            layer, 0, red_src.at[layer, some], red_in.at[layer, some], near_device(lax.rem(me_n + 1, n_near))
        ).wait()
        red_in[layer, me_n] = red_src[layer, me_n]
        red_z[layer, far] = jnp.sum(red_in[layer].astype(F32), axis=0).astype(BF16)

        def go(j, carry):
            t = lax.rem(far + j, n_far)
            all_copy(layer, 1, red_z.at[layer, far], red_z.at[layer, far], (me_q, t * grp + near)).start()
            return carry

        loop(1, n_far, go)

    def gather_start(layer):
        if n_far > 1:
            some = pl.ds(0, n_far - 1)
            all_copy(
                layer,
                1,
                red_z.at[layer, some],
                red_z.at[layer, some],
                (me_q, lax.rem(far + 1, n_far) * grp + near),
            ).wait()
        red_all[layer, me_n] = jnp.sum(red_z[layer].astype(F32), axis=0).astype(BF16)

        def go(j, carry):
            t = lax.rem(me_n + j, n_near)
            all_copy(layer, 2, red_all.at[layer, me_n], red_all.at[layer, me_n], near_device(t)).start()
            return carry

        loop(1, n_near, go)

    def gather_wait(layer):
        some = pl.ds(0, n_near - 1)
        all_copy(
            layer, 2, red_all.at[layer, some], red_all.at[layer, some], near_device(lax.rem(me_n + 1, n_near))
        ).wait()

    def pack(layer, rg, wg):
        parts = [rg, wg]
        left = width - rel_rows - feat
        if left:
            parts.append(jnp.zeros((feat, left), F32))
        whole = jnp.concatenate(parts, axis=1)
        red_src[layer] = whole.reshape(n_near, feat // n_near, width).astype(BF16)

    def unpack(layer):
        summed = red_all[layer].astype(F32).reshape(feat, width)
        grel_ref[layer] = summed[:, :rel_count] * scale_r
        gw_ref[layer] = summed[:, rel_rows : rel_rows + feat] * scale_w

    per = 128 // send
    spread = jnp.concatenate([gs_ref[...]] * per, axis=1)
    for p in range(n_d):
        gs_x[p] = spread[p : p + 1, :]

    onehot_into(vt, ein_ref[1:2, :], 0, 64)
    onehot_into(vt, ebd_ref[1:2, :], e_in, 64)
    pl.semaphore_wait(barrier, greeted)
    exchange_start(0, gs_x, req, None)
    onehot_into(st_in, ein_ref[0:1, :], 0, 64)
    onehot_into(st_bd, ebd_ref[0:1, :], 0, 64)

    slots = bnd_ref.shape[1]
    own_ids = lax.broadcasted_iota(jnp.int32, (rows, slots), 0)
    row_of32 = jnp.where(own_ids == bnd_ref[...], 1.0, 0.0)
    row_of = row_of32.astype(BF16)
    published = dot_nn(row_of32.T.astype(BF16), h_ref[...]).astype(BF16)

    exchange_wait(0, gs_x, req, None)
    lane_group = lax.broadcasted_iota(jnp.int32, (1, 128), 1) // send
    wanted = []
    for j in range(n_d // per):
        vec = jnp.zeros((1, 128), jnp.int32)
        for k in range(per):
            vec = jnp.where(lane_group == k, req[j * per + k, 0:1, :], vec)
        wanted.append(vec)
    wanted = jnp.concatenate(wanted, axis=1)
    slot_ids = lax.broadcasted_iota(jnp.int32, (slots, n_d * send), 0)
    slot_of32 = jnp.where(slot_ids == wanted, 1.0, 0.0)
    slot_of_t = slot_of32.T.astype(BF16)
    out1[...] = dot_nn(slot_of_t, published).astype(BF16)
    exchange_start(1, out1, ghost1, send)

    onehot_into(rt, ein_ref[2:3, :], 0, 32)
    onehot_into(rt, ebd_ref[2:3, :], e_in, 32)
    relt[...] = jnp.zeros_like(relt)
    relt[pl.ds(0, feat), pl.ds(0, rel_count)] = r1_ref[...]
    relt[pl.ds(feat, feat), pl.ds(0, rel_count)] = r2_ref[...]
    rel_e[...] = dot_nn(relt[...], rt[...]).astype(BF16)
    pick_t = dot_nn(row_of, slot_of32.astype(BF16)).astype(BF16)
    pick = dot_nt(slot_of_t, row_of).astype(BF16)

    row_ids = lax.broadcasted_iota(jnp.int32, (feat, rows), 1) + me_d * rows
    lane_rel = lax.broadcasted_iota(jnp.int32, (feat, rel_count), 1)
    qtab = qe_ref[...].astype(F32)
    boost_parts = []
    for q in range(queries):
        vec = jnp.sum(jnp.where(lane_rel == qrel_ref[q], qtab, 0.0), axis=1, keepdims=True)
        boost_parts.append(jnp.where(row_ids == qhead_ref[q], vec, 0.0))
    boost = jnp.concatenate(boost_parts, axis=0)

    h32 = h_ref[...].astype(F32)
    h_t32 = h32.T
    h_t = h_t32.astype(BF16)

    def rel_tile(layer, lo, count):
        part = rel_e[pl.ds(layer * feat, feat), pl.ds(lo, count)].astype(F32)
        return jnp.concatenate([part] * queries, axis=0)

    def aggregate(layer, table_t, onehot, save, lo, count):
        sourced = dot_nn(table_t, onehot[...])
        save[:, pl.ds(lo, count)] = sourced.astype(BF16)
        message = split_hi_lo(sourced * rel_tile(layer, lo, count), 0)
        both = dot_nt(message, vt[:, pl.ds(lo, count)])
        return both[:wide] + both[wide:]

    def normalise(summed, w_ref):
        summed_b = summed.astype(BF16)
        normed, rstds = [], []
        for q in range(queries):
            mixed = lax.dot_general(
                w_ref[...],
                summed_b[q * feat : (q + 1) * feat],
                (((0,), (0,)), ((), ())),
                preferred_element_type=F32,
            )
            center = mixed - jnp.mean(mixed, axis=0, keepdims=True)
            rstd = lax.rsqrt(jnp.mean(center * center, axis=0, keepdims=True) + 1e-05)
            normed.append(center * rstd)
            rstds.append(rstd)
        return summed_b, normed, rstds

    def silu_slope(y):
        sig = jax.nn.sigmoid(y)
        return sig * (1.0 + y * (1.0 - sig))

    def back_layer(up_t, slopes, normed, rstds, w_ref):
        dmixes, dsum = [], []
        for q in range(queries):
            y = normed[q]
            dact = up_t[q * feat : (q + 1) * feat] * slopes[q]
            dmix = rstds[q] * (
                dact
                - jnp.mean(dact, axis=0, keepdims=True)
                - y * jnp.mean(dact * y, axis=0, keepdims=True)
            )
            dmix_b = dmix.astype(BF16)
            dmixes.append(dmix_b)
            dsum.append(dot_nn(w_ref[...], dmix_b).astype(BF16))
        return dmixes, jnp.concatenate(dsum, axis=0)

    def weight_grad(summed_b, dmixes):
        wgrad = jnp.zeros((feat, feat), F32)
        for q in range(queries):
            wgrad = wgrad + dot_nt(summed_b[q * feat : (q + 1) * feat], dmixes[q])
        return wgrad

    def rel_grad(downs, save):
        tots = []
        lo = 0
        for down in downs:
            count = down.shape[1]
            prod = down * save[:, pl.ds(lo, count)].astype(F32)
            tot = prod[:feat]
            for q in range(1, queries):
                tot = tot + prod[q * feat : (q + 1) * feat]
            tots.append(split_hi_lo(tot, 0))
            lo += count
        both = dot_nt(jnp.concatenate(tots, axis=1), rt[pl.ds(0, rel_rows), :])
        return both[:feat] + both[feat:]

    def table_grad(layer, down, onehot, lo, count):
        part = rel_e[pl.ds(layer * feat, feat), pl.ds(lo, count)]
        message = down.astype(BF16) * jnp.concatenate([part] * queries, axis=0)
        return dot_nt(onehot[...], message)

    def give_back(ret_in):
        return dot_nn(pick_t, ret_in[...])

    sum1 = aggregate(0, h_t, st_in, x1, 0, e_in) + boost
    exchange_wait(1, out1, ghost1, send)
    sum1 = sum1 + aggregate(0, ghost1[...].astype(F32).T.astype(BF16), st_bd, x1, e_in, e_bd)
    sum1_b, norm1, rstd1 = normalise(sum1, w1_ref)
    h2_t = (
        jnp.concatenate([y * jax.nn.sigmoid(y) for y in norm1], axis=0) + h_t32
    ).astype(BF16)

    out2[...] = dot_nt(pick, h2_t).astype(BF16)
    exchange_start(2, out2, ghost2, send)
    sum2 = aggregate(1, h2_t, st_in, x2, 0, e_in) + boost
    cot32 = cot_ref[...].astype(F32)
    cot_t[...] = cot32.T
    for q in range(queries):
        slope1[pl.ds(q * feat, feat), :] = silu_slope(norm1[q])
    exchange_wait(2, out2, ghost2, send)
    sum2 = sum2 + aggregate(1, ghost2[...].astype(F32).T.astype(BF16), st_bd, x2, e_in, e_bd)
    sum2_b, norm2, rstd2 = normalise(sum2, w2_ref)

    dmix2, dsum2 = back_layer(cot_t[...], [silu_slope(y) for y in norm2], norm2, rstd2, w2_ref)
    down2_bd = dot_nn(dsum2, vt[:, pl.ds(e_in, e_bd)])
    ret_out2[...] = table_grad(1, down2_bd, st_bd, e_in, e_bd).astype(BF16)
    exchange_start(3, ret_out2, ret_in2, send)
    down2_in = dot_nn(dsum2, vt[:, pl.ds(0, e_in)])
    pack(1, rel_grad((down2_in, down2_bd), x2), weight_grad(sum2_b, dmix2))
    scatter_start(1)
    mid = cot32 + table_grad(1, down2_in, st_in, 0, e_in)
    exchange_wait(3, ret_out2, ret_in2, send)
    mid = mid + give_back(ret_in2)

    slopes1 = [slope1[pl.ds(q * feat, feat), :] for q in range(queries)]
    dmix1, dsum1 = back_layer(mid.T, slopes1, norm1, rstd1, w1_ref)
    down1_in = dot_nn(dsum1, vt[:, pl.ds(0, e_in)])
    down1_bd = dot_nn(dsum1, vt[:, pl.ds(e_in, e_bd)])
    pack(0, rel_grad((down1_in, down1_bd), x1), weight_grad(sum1_b, dmix1))
    scatter_start(0)
    far_start(1)
    ret_out1[...] = table_grad(0, down1_bd, st_bd, e_in, e_bd).astype(BF16)
    exchange_start(4, ret_out1, ret_in1, send)
    base = mid + table_grad(0, down1_in, st_in, 0, e_in)
    far_start(0)
    gather_start(1)
    exchange_wait(4, ret_out1, ret_in1, send)
    gin_ref[...] = base + give_back(ret_in1)
    gather_start(0)
    gather_wait(1)
    unpack(1)
    gather_wait(0)
    unpack(0)


def write_out(*refs):
    half = (len(refs) - 1) // 2
    copies = [
        pltpu.make_async_copy(src, dst, refs[-1].at[k])
        for k, (src, dst) in enumerate(zip(refs[:half], refs[half : 2 * half]))
    ]
    for copy in copies:
        copy.start()
    for copy in copies:
        copy.wait()


def body(
    h_in,
    cotangent,
    w_one,
    w_two,
    rel_one,
    rel_two,
    query_emb,
    q_head,
    q_rel,
    bnd_rows,
    ghost_slots,
    edges_in,
    edges_bd,
):
    rows, wide = h_in.shape
    feat = w_one.shape[0]
    queries = wide // feat
    rel_count = rel_one.shape[0]
    n_d = lax.axis_size("dom")
    n_q = lax.axis_size("query")
    send = ghost_slots.shape[1]
    ghosts = n_d * send
    e_in, e_bd = edges_in.shape[1], edges_bd.shape[1]
    edges = e_in + e_bd
    rel_pad = -(-(rel_count + 1) // 128) * 128
    rel_rows = -(-(rel_count + 1) // 16) * 16
    width = -(-(rel_rows + feat) // 128) * 128
    grp = max(1, 8 // n_q)
    n_near, n_far = n_q * grp, n_d // grp
    part = feat // n_near
    scale_w = 1.0 / math.sqrt(rows * n_d * queries * n_q)
    scale_r = math.sqrt(rel_count / (n_d * edges * queries * n_q))

    args = (
        h_in,
        cotangent,
        w_one,
        w_two,
        rel_one.T,
        rel_two.T,
        query_emb.T,
        q_head,
        q_rel,
        bnd_rows[None, :],
        ghost_slots,
        edges_in,
        edges_bd,
    )
    spaces = [pltpu.VMEM] * 7 + [pltpu.SMEM] * 2 + [pltpu.VMEM] * 4

    vmem = pl.BlockSpec(memory_space=pltpu.VMEM)
    dma = pltpu.SemaphoreType.DMA
    shapes = (
        jax.ShapeDtypeStruct((rows, wide), F32),
        jax.ShapeDtypeStruct((2, feat, feat), F32),
        jax.ShapeDtypeStruct((2, feat, rel_count), F32),
    )
    results = pl.pallas_call(
        functools.partial(kernel, n_q, n_d, grp, scale_w, scale_r, rel_count, rel_rows),
        out_shape=tuple(pltpu.VMEM(s.shape, s.dtype) for s in shapes),
        in_specs=[pl.BlockSpec(memory_space=pltpu.HBM)] * len(args),
        out_specs=(vmem, vmem, vmem),
        scratch_shapes=[
            *(space(a.shape, a.dtype) for a, space in zip(args, spaces)),
            pltpu.VMEM((2 * feat, rel_pad), BF16),
            pltpu.VMEM((n_d, 1, 128), jnp.int32),
            pltpu.VMEM((rel_pad, edges), BF16),
            pltpu.VMEM((rows, edges), BF16),
            pltpu.VMEM((rows, e_in), BF16),
            pltpu.VMEM((ghosts, e_bd), BF16),
            pltpu.VMEM((2 * feat, edges), BF16),
            pltpu.VMEM((wide, edges), BF16),
            pltpu.VMEM((wide, edges), BF16),
            pltpu.VMEM((n_d, 1, 128), jnp.int32),
            pltpu.VMEM((ghosts, wide), BF16),
            pltpu.VMEM((ghosts, wide), BF16),
            pltpu.VMEM((ghosts, wide), BF16),
            pltpu.VMEM((ghosts, wide), BF16),
            pltpu.VMEM((ghosts, wide), BF16),
            pltpu.VMEM((ghosts, wide), BF16),
            pltpu.VMEM((ghosts, wide), BF16),
            pltpu.VMEM((ghosts, wide), BF16),
            pltpu.VMEM((wide, rows), F32),
            pltpu.VMEM((wide, rows), F32),
            pltpu.VMEM((2, n_near, part, width), BF16),
            pltpu.VMEM((2, n_near, part, width), BF16),
            pltpu.VMEM((2, n_far, part, width), BF16),
            pltpu.VMEM((2, n_near, part, width), BF16),
            dma((5,)),
            dma((5,)),
            dma((2, 3)),
            dma((2, 3)),
            dma((len(args),)),
        ],
        compiler_params=pltpu.CompilerParams(
            collective_id=0, has_side_effects=True, vmem_limit_bytes=33554432
        ),
    )(*(pltpu.with_memory_space_constraint(a, pltpu.HBM) for a in args))
    grad_in, grad_w, grad_rel_t = pl.pallas_call(
        write_out,
        out_shape=shapes,
        in_specs=[vmem] * 3,
        out_specs=[pl.BlockSpec(memory_space=pltpu.HBM)] * 3,
        scratch_shapes=[dma((3,))],
        compiler_params=pltpu.CompilerParams(vmem_limit_bytes=16777216),
    )(*results)
    return grad_in, grad_w, jnp.swapaxes(grad_rel_t, 1, 2)


def solution(mesh):
    return jax.shard_map(
        body,
        mesh=mesh,
        in_specs=(
            P("dom", "query"),
            P("dom", "query"),
            P(),
            P(),
            P(),
            P(),
            P(),
            P("query"),
            P("query"),
            P("dom"),
            P("dom", None),
            P(None, "dom"),
            P(None, "dom"),
        ),
        out_specs=(P("dom", "query"), P(), P()),
        check_vma=False,
    )
```

```python
import functools
import math

import jax
import jax.numpy as jnp
from jax import lax
from jax.experimental import pallas as pl
from jax.experimental.pallas import tpu as pltpu
from jax.sharding import PartitionSpec as P

MESH = pl.DeviceIdType.MESH
F32 = jnp.float32
BF16 = jnp.bfloat16


def dot_nn(a, b):
    return lax.dot_general(a, b, (((1,), (0,)), ((), ())), preferred_element_type=F32)


def dot_nt(a, b):
    return lax.dot_general(a, b, (((1,), (1,)), ((), ())), preferred_element_type=F32)


def split_hi_lo(x, axis):
    hi = x.astype(BF16)
    lo = (x - hi.astype(F32)).astype(BF16)
    return jnp.concatenate([hi, lo], axis=axis)


def onehot_into(dest, ids, col0, block):
    rows = dest.shape[0]
    count = ids.shape[1]

    def fill(i, carry):
        base = pl.multiple_of(i * block, block)
        row_ids = lax.broadcasted_iota(jnp.int32, (block, count), 0) + base
        dest[pl.ds(base, block), pl.ds(col0, count)] = jnp.where(row_ids == ids, 1.0, 0.0).astype(BF16)
        return carry

    lax.fori_loop(0, rows // block, fill, 0)


def loop(low, high, step):
    if high - low <= 32:
        for i in range(low, high):
            step(i, 0)
    else:
        lax.fori_loop(low, high, step, 0)


def div(a, b):
    return a // b if isinstance(a, int) else lax.div(a, b)


def rem(a, b):
    return a % b if isinstance(a, int) else lax.rem(a, b)


def aligned(a, b):
    return a if isinstance(a, int) else pl.multiple_of(a, b)


def kernel(
    n_q,
    n_d,
    grp,
    scale_w,
    scale_r,
    rel_count,
    rel_rows,
    *refs,
):
    n_in = 13
    hbm = refs[:n_in]
    gin_ref, gw_ref, grel_ref = refs[n_in : n_in + 3]
    local = refs[n_in + 3 : 2 * n_in + 3]
    (
        h_ref, cot_ref, w1_ref, w2_ref, r1_ref, r2_ref, qe_ref, qhead_ref, qrel_ref, bnd_ref, gs_ref, ein_ref, ebd_ref,
    ) = local
    (
    relt,
    gs_x,
    rt,
    vt,
    st_in,
    st_bd,
    rel_e,
    x1,
    x2,
    req,
    out1,
    ghost1,
    out2,
    ghost2,
    ret_out2,
    ret_in2,
    ret_out1,
    ret_in1,
    red_src,
    red_in,
    red_z,
    red_all,
    xsend,
    xrecv,
    asend,
    arecv,
    load_sem,
    ) = refs[2 * n_in + 3 :]
    me_d = lax.axis_index("dom")
    me_q = lax.axis_index("query")
    n_far = n_d // grp
    n_near = n_q * grp
    far = lax.div(me_d, grp)
    near = lax.rem(me_d, grp)
    me_n = me_q * grp + near
    feat = w1_ref.shape[0]
    rows, wide = h_ref.shape
    queries = wide // feat
    send = ghost1.shape[0] // n_d
    e_in = ein_ref.shape[1]
    e_bd = ebd_ref.shape[1]
    width = red_src.shape[3]

    def peer_loop(step):
        if n_d <= 32:
            order = sorted(range(1, n_d), key=lambda i: -min(i // grp, n_far - i // grp))
            for i in order:
                step(i, 0)
        else:
            lax.fori_loop(1, n_d, step, 0)

    barrier = pltpu.get_barrier_semaphore()

    def greet(i, carry):
        t = lax.rem(me_d + i, n_d)
        pl.semaphore_signal(barrier, inc=1, device_id=(me_q, t), device_id_type=MESH)
        return carry

    peer_loop(greet)
    for dq in range(1, n_q):
        for k in range(grp):
            pl.semaphore_signal(
                barrier,
                inc=1,
                device_id=(lax.rem(me_q + dq, n_q), far * grp + k),
                device_id_type=MESH,
            )
    greeted = n_d - 1 + (n_q - 1) * grp
    loads = [
        pltpu.make_async_copy(src, dst, load_sem.at[k])
        for k, (src, dst) in enumerate(zip(hbm, local))
    ]
    for load in loads[::-1]:
        load.start()
    for load in loads[10:]:
        load.wait()

    def exchange_start(phase, src, dst, size):
        def go(i, carry):
            peer = lax.rem(me_d + i, n_d)
            if size is None:
                s, d = src.at[peer], dst.at[me_d]
            else:
                s = src.at[pl.ds(pl.multiple_of(peer * size, size), size)]
                d = dst.at[pl.ds(pl.multiple_of(me_d * size, size), size)]
            pltpu.make_async_remote_copy(
                src_ref=s,
                dst_ref=d,
                send_sem=xsend.at[phase],
                recv_sem=xrecv.at[phase],
                device_id=(me_q, peer),
                device_id_type=MESH,
            ).start()
            return carry

        peer_loop(go)
        if size is None:
            dst[me_d] = src[me_d]
        else:
            own = pl.ds(pl.multiple_of(me_d * size, size), size)
            dst[own, :] = src[own, :]

    def exchange_wait(phase, src, dst, size):
        some = pl.ds(0, (n_d - 1) * (size or 1))
        pltpu.make_async_remote_copy(
            src_ref=src.at[some],
            dst_ref=dst.at[some],
            send_sem=xsend.at[phase],
            recv_sem=xrecv.at[phase],
            device_id=(me_q, lax.rem(me_d + 1, n_d)),
            device_id_type=MESH,
        ).wait()

    def near_device(t):
        return lax.div(t, grp), far * grp + lax.rem(t, grp)

    def all_copy(layer, stage, src, dst, device):
        return pltpu.make_async_remote_copy(
            src_ref=src,
            dst_ref=dst,
            send_sem=asend.at[layer, stage],
            recv_sem=arecv.at[layer, stage],
            device_id=device,
            device_id_type=MESH,
        )

    def scatter_start(layer):
        def go(j, carry):
            t = lax.rem(me_n + j, n_near)
            all_copy(layer, 0, red_src.at[layer, t], red_in.at[layer, me_n], near_device(t)).start()
            return carry

        loop(1, n_near, go)

    def far_start(layer):
        some = pl.ds(0, n_near - 1)
        all_copy(
            layer, 0, red_src.at[layer, some], red_in.at[layer, some], near_device(lax.rem(me_n + 1, n_near))
        ).wait()
        red_in[layer, me_n] = red_src[layer, me_n]
        red_z[layer, far] = jnp.sum(red_in[layer].astype(F32), axis=0).astype(BF16)

        def go(j, carry):
            t = lax.rem(far + j, n_far)
            all_copy(layer, 1, red_z.at[layer, far], red_z.at[layer, far], (me_q, t * grp + near)).start()
            return carry

        loop(1, n_far, go)

    def gather_start(layer):
        if n_far > 1:
            some = pl.ds(0, n_far - 1)
            all_copy(
                layer,
                1,
                red_z.at[layer, some],
                red_z.at[layer, some],
                (me_q, lax.rem(far + 1, n_far) * grp + near),
            ).wait()
        red_all[layer, me_n] = jnp.sum(red_z[layer].astype(F32), axis=0).astype(BF16)

        def go(j, carry):
            t = lax.rem(me_n + j, n_near)
            all_copy(layer, 2, red_all.at[layer, me_n], red_all.at[layer, me_n], near_device(t)).start()
            return carry

        loop(1, n_near, go)

    def gather_wait(layer):
        some = pl.ds(0, n_near - 1)
        all_copy(
            layer, 2, red_all.at[layer, some], red_all.at[layer, some], near_device(lax.rem(me_n + 1, n_near))
        ).wait()

    def pack(layer, rg, wg):
        parts = [rg, wg]
        left = width - rel_rows - feat
        if left:
            parts.append(jnp.zeros((feat, left), F32))
        whole = jnp.concatenate(parts, axis=1)
        red_src[layer] = whole.reshape(n_near, feat // n_near, width).astype(BF16)

    def unpack(layer):
        summed = red_all[layer].astype(F32).reshape(feat, width)
        grel_ref[layer] = summed[:, :rel_count] * scale_r
        gw_ref[layer] = summed[:, rel_rows : rel_rows + feat] * scale_w

    per = 128 // send
    spread = jnp.concatenate([gs_ref[...]] * per, axis=1)
    for p in range(n_d):
        gs_x[p] = spread[p : p + 1, :]

    onehot_into(vt, ein_ref[1:2, :], 0, 64)
    onehot_into(vt, ebd_ref[1:2, :], e_in, 64)
    pl.semaphore_wait(barrier, greeted)
    exchange_start(0, gs_x, req, None)
    for load in loads[:10]:
        load.wait()
    onehot_into(st_in, ein_ref[0:1, :], 0, 64)
    onehot_into(st_bd, ebd_ref[0:1, :], 0, 64)

    slots = bnd_ref.shape[1]
    own_ids = lax.broadcasted_iota(jnp.int32, (rows, slots), 0)
    row_of32 = jnp.where(own_ids == bnd_ref[...], 1.0, 0.0)
    row_of = row_of32.astype(BF16)
    published = dot_nn(row_of32.T.astype(BF16), h_ref[...]).astype(BF16)

    exchange_wait(0, gs_x, req, None)
    lane_group = lax.broadcasted_iota(jnp.int32, (1, 128), 1) // send
    wanted = []
    for j in range(n_d // per):
        vec = jnp.zeros((1, 128), jnp.int32)
        for k in range(per):
            vec = jnp.where(lane_group == k, req[j * per + k, 0:1, :], vec)
        wanted.append(vec)
    wanted = jnp.concatenate(wanted, axis=1)
    slot_ids = lax.broadcasted_iota(jnp.int32, (slots, n_d * send), 0)
    slot_of32 = jnp.where(slot_ids == wanted, 1.0, 0.0)
    slot_of_t = slot_of32.T.astype(BF16)
    out1[...] = dot_nn(slot_of_t, published).astype(BF16)
    exchange_start(1, out1, ghost1, send)

    onehot_into(rt, ein_ref[2:3, :], 0, 32)
    onehot_into(rt, ebd_ref[2:3, :], e_in, 32)
    relt[...] = jnp.zeros_like(relt)
    relt[pl.ds(0, feat), pl.ds(0, rel_count)] = r1_ref[...]
    relt[pl.ds(feat, feat), pl.ds(0, rel_count)] = r2_ref[...]
    rel_e[...] = dot_nn(relt[...], rt[...]).astype(BF16)
    pick_t = dot_nn(row_of, slot_of32.astype(BF16)).astype(BF16)
    pick = dot_nt(slot_of_t, row_of).astype(BF16)

    row_ids = lax.broadcasted_iota(jnp.int32, (feat, rows), 1) + me_d * rows
    lane_rel = lax.broadcasted_iota(jnp.int32, (feat, rel_count), 1)
    qtab = qe_ref[...].astype(F32)
    boost_parts = []
    for q in range(queries):
        vec = jnp.sum(jnp.where(lane_rel == qrel_ref[q], qtab, 0.0), axis=1, keepdims=True)
        boost_parts.append(jnp.where(row_ids == qhead_ref[q], vec, 0.0))
    boost = jnp.concatenate(boost_parts, axis=0)

    h32 = h_ref[...].astype(F32)
    h_t32 = h32.T
    h_t = h_t32.astype(BF16)

    def rel_tile(layer, lo, count):
        part = rel_e[pl.ds(layer * feat, feat), pl.ds(lo, count)].astype(F32)
        return jnp.concatenate([part] * queries, axis=0)

    def aggregate(layer, table_t, onehot, save, lo, count):
        sourced = dot_nn(table_t, onehot[...])
        save[:, pl.ds(lo, count)] = sourced.astype(BF16)
        message = split_hi_lo(sourced * rel_tile(layer, lo, count), 0)
        both = dot_nt(message, vt[:, pl.ds(lo, count)])
        return both[:wide] + both[wide:]

    def normalise(summed, w_ref):
        summed_b = summed.astype(BF16)
        normed, rstds = [], []
        for q in range(queries):
            mixed = lax.dot_general(
                w_ref[...],
                summed_b[q * feat : (q + 1) * feat],
                (((0,), (0,)), ((), ())),
                preferred_element_type=F32,
            )
            center = mixed - jnp.mean(mixed, axis=0, keepdims=True)
            rstd = lax.rsqrt(jnp.mean(center * center, axis=0, keepdims=True) + 1e-05)
            normed.append(center * rstd)
            rstds.append(rstd)
        return summed_b, normed, rstds

    def back_layer(up_t, normed, rstds, w_ref):
        dmixes, dsum = [], []
        for q in range(queries):
            y = normed[q]
            sig = jax.nn.sigmoid(y)
            dact = up_t[q * feat : (q + 1) * feat] * sig * (1.0 + y * (1.0 - sig))
            dmix = rstds[q] * (
                dact
                - jnp.mean(dact, axis=0, keepdims=True)
                - y * jnp.mean(dact * y, axis=0, keepdims=True)
            )
            dmix_b = dmix.astype(BF16)
            dmixes.append(dmix_b)
            dsum.append(dot_nn(w_ref[...], dmix_b).astype(BF16))
        return dmixes, jnp.concatenate(dsum, axis=0)

    def weight_grad(summed_b, dmixes):
        wgrad = jnp.zeros((feat, feat), F32)
        for q in range(queries):
            wgrad = wgrad + dot_nt(summed_b[q * feat : (q + 1) * feat], dmixes[q])
        return wgrad

    def rel_grad(downs, save):
        tots = []
        lo = 0
        for down in downs:
            count = down.shape[1]
            prod = down * save[:, pl.ds(lo, count)].astype(F32)
            tot = prod[:feat]
            for q in range(1, queries):
                tot = tot + prod[q * feat : (q + 1) * feat]
            tots.append(tot.astype(BF16))
            lo += count
        return dot_nt(jnp.concatenate(tots, axis=1), rt[pl.ds(0, rel_rows), :])

    def table_grad(layer, down, onehot, lo, count):
        message = (down * rel_tile(layer, lo, count)).astype(BF16)
        return dot_nt(onehot[...], message)

    def give_back(ret_in):
        return dot_nn(pick_t, ret_in[...])

    sum1 = aggregate(0, h_t, st_in, x1, 0, e_in) + boost
    exchange_wait(1, out1, ghost1, send)
    sum1 = sum1 + aggregate(0, ghost1[...].astype(F32).T.astype(BF16), st_bd, x1, e_in, e_bd)
    sum1_b, norm1, rstd1 = normalise(sum1, w1_ref)
    h2_t = (
        jnp.concatenate([y * jax.nn.sigmoid(y) for y in norm1], axis=0) + h_t32
    ).astype(BF16)

    out2[...] = dot_nt(pick, h2_t).astype(BF16)
    exchange_start(2, out2, ghost2, send)
    sum2 = aggregate(1, h2_t, st_in, x2, 0, e_in) + boost
    exchange_wait(2, out2, ghost2, send)
    sum2 = sum2 + aggregate(1, ghost2[...].astype(F32).T.astype(BF16), st_bd, x2, e_in, e_bd)
    sum2_b, norm2, rstd2 = normalise(sum2, w2_ref)

    cot32 = cot_ref[...].astype(F32)
    dmix2, dsum2 = back_layer(cot32.T, norm2, rstd2, w2_ref)
    down2_bd = dot_nn(dsum2, vt[:, pl.ds(e_in, e_bd)])
    ret_out2[...] = table_grad(1, down2_bd, st_bd, e_in, e_bd).astype(BF16)
    exchange_start(3, ret_out2, ret_in2, send)
    down2_in = dot_nn(dsum2, vt[:, pl.ds(0, e_in)])
    pack(1, rel_grad((down2_in, down2_bd), x2), weight_grad(sum2_b, dmix2))
    scatter_start(1)
    mid = cot32 + table_grad(1, down2_in, st_in, 0, e_in)
    exchange_wait(3, ret_out2, ret_in2, send)
    mid = mid + give_back(ret_in2)

    dmix1, dsum1 = back_layer(mid.T, norm1, rstd1, w1_ref)
    down1_in = dot_nn(dsum1, vt[:, pl.ds(0, e_in)])
    down1_bd = dot_nn(dsum1, vt[:, pl.ds(e_in, e_bd)])
    pack(0, rel_grad((down1_in, down1_bd), x1), weight_grad(sum1_b, dmix1))
    scatter_start(0)
    far_start(1)
    ret_out1[...] = table_grad(0, down1_bd, st_bd, e_in, e_bd).astype(BF16)
    exchange_start(4, ret_out1, ret_in1, send)
    base = mid + table_grad(0, down1_in, st_in, 0, e_in)
    far_start(0)
    gather_start(1)
    exchange_wait(4, ret_out1, ret_in1, send)
    gin_ref[...] = base + give_back(ret_in1)
    gather_start(0)
    gather_wait(1)
    unpack(1)
    gather_wait(0)
    unpack(0)


def write_out(*refs):
    half = (len(refs) - 1) // 2
    copies = [
        pltpu.make_async_copy(src, dst, refs[-1].at[k])
        for k, (src, dst) in enumerate(zip(refs[:half], refs[half : 2 * half]))
    ]
    for copy in copies:
        copy.start()
    for copy in copies:
        copy.wait()


def body(
    h_in,
    cotangent,
    w_one,
    w_two,
    rel_one,
    rel_two,
    query_emb,
    q_head,
    q_rel,
    bnd_rows,
    ghost_slots,
    edges_in,
    edges_bd,
):
    rows, wide = h_in.shape
    feat = w_one.shape[0]
    queries = wide // feat
    rel_count = rel_one.shape[0]
    n_d = lax.axis_size("dom")
    n_q = lax.axis_size("query")
    send = ghost_slots.shape[1]
    ghosts = n_d * send
    e_in, e_bd = edges_in.shape[1], edges_bd.shape[1]
    edges = e_in + e_bd
    rel_pad = -(-(rel_count + 1) // 128) * 128
    rel_rows = -(-(rel_count + 1) // 16) * 16
    width = -(-(rel_rows + feat) // 128) * 128
    grp = max(1, 8 // n_q)
    n_near, n_far = n_q * grp, n_d // grp
    part = feat // n_near
    scale_w = 1.0 / math.sqrt(rows * n_d * queries * n_q)
    scale_r = math.sqrt(rel_count / (n_d * edges * queries * n_q))

    args = (
        h_in,
        cotangent,
        w_one,
        w_two,
        rel_one.T,
        rel_two.T,
        query_emb.T,
        q_head,
        q_rel,
        bnd_rows[None, :],
        ghost_slots,
        edges_in,
        edges_bd,
    )
    spaces = [pltpu.VMEM] * 7 + [pltpu.SMEM] * 2 + [pltpu.VMEM] * 4

    vmem = pl.BlockSpec(memory_space=pltpu.VMEM)
    dma = pltpu.SemaphoreType.DMA
    shapes = (
        jax.ShapeDtypeStruct((rows, wide), F32),
        jax.ShapeDtypeStruct((2, feat, feat), F32),
        jax.ShapeDtypeStruct((2, feat, rel_count), F32),
    )
    results = pl.pallas_call(
        functools.partial(kernel, n_q, n_d, grp, scale_w, scale_r, rel_count, rel_rows),
        out_shape=tuple(pltpu.VMEM(s.shape, s.dtype) for s in shapes),
        in_specs=[pl.BlockSpec(memory_space=pltpu.HBM)] * len(args),
        out_specs=(vmem, vmem, vmem),
        scratch_shapes=[
            *(space(a.shape, a.dtype) for a, space in zip(args, spaces)),
            pltpu.VMEM((2 * feat, rel_pad), BF16),
            pltpu.VMEM((n_d, 1, 128), jnp.int32),
            pltpu.VMEM((rel_pad, edges), BF16),
            pltpu.VMEM((rows, edges), BF16),
            pltpu.VMEM((rows, e_in), BF16),
            pltpu.VMEM((ghosts, e_bd), BF16),
            pltpu.VMEM((2 * feat, edges), BF16),
            pltpu.VMEM((wide, edges), BF16),
            pltpu.VMEM((wide, edges), BF16),
            pltpu.VMEM((n_d, 1, 128), jnp.int32),
            pltpu.VMEM((ghosts, wide), BF16),
            pltpu.VMEM((ghosts, wide), BF16),
            pltpu.VMEM((ghosts, wide), BF16),
            pltpu.VMEM((ghosts, wide), BF16),
            pltpu.VMEM((ghosts, wide), BF16),
            pltpu.VMEM((ghosts, wide), BF16),
            pltpu.VMEM((ghosts, wide), BF16),
            pltpu.VMEM((ghosts, wide), BF16),
            pltpu.VMEM((2, n_near, part, width), BF16),
            pltpu.VMEM((2, n_near, part, width), BF16),
            pltpu.VMEM((2, n_far, part, width), BF16),
            pltpu.VMEM((2, n_near, part, width), BF16),
            dma((5,)),
            dma((5,)),
            dma((2, 3)),
            dma((2, 3)),
            dma((len(args),)),
        ],
        compiler_params=pltpu.CompilerParams(
            collective_id=0, has_side_effects=True, vmem_limit_bytes=33554432
        ),
    )(*(pltpu.with_memory_space_constraint(a, pltpu.HBM) for a in args))
    grad_in, grad_w, grad_rel_t = pl.pallas_call(
        write_out,
        out_shape=shapes,
        in_specs=[vmem] * 3,
        out_specs=[pl.BlockSpec(memory_space=pltpu.HBM)] * 3,
        scratch_shapes=[dma((3,))],
        compiler_params=pltpu.CompilerParams(vmem_limit_bytes=16777216),
    )(*results)
    return grad_in, grad_w, jnp.swapaxes(grad_rel_t, 1, 2)


def solution(mesh):
    return jax.shard_map(
        body,
        mesh=mesh,
        in_specs=(
            P("dom", "query"),
            P("dom", "query"),
            P(),
            P(),
            P(),
            P(),
            P(),
            P("query"),
            P("query"),
            P("dom"),
            P("dom", None),
            P(None, "dom"),
            P(None, "dom"),
        ),
        out_specs=(P("dom", "query"), P(), P()),
        check_vma=False,
    )
```
